32 devices in a mesh: lev: 4 (over x, core), gy: 8 (over z, y).
Axes of the slice: x: 2, y: 2, z: 4, core: 2. Of those that a mesh axis runs over, the one named last changes fastest.
Arguments:
- forcing: bfloat16 [4, 32, 768, 1024], P('lev', None, 'gy'), may hold values from -6 to 6
- spectral_weight: bfloat16 [2, 128, 32, 32, 128], P(None, 'gy'), may hold values from -4.1875 to 4.1875
- point_weight: bfloat16 [32, 32], replicated, may hold values from -1 to 1
- point_bias: float32 [32], replicated, may hold values from -3 to 3
- decoder: bfloat16 [4, 32], replicated, may hold values from -1 to 1
- coriolis: float32 [768], P('gy'), may hold values from -1.5 to 1.5
- layer_depth: float32 [4], replicated, may hold values from 0.5 to 2
Outputs:
- equilibrium: float32 [4, 32, 768, 1024], P('lev', None, 'gy')
- residual: float32 [3, 4, 768, 1024], P(None, 'lev', 'gy')
The draws below stay inside these ranges and needn't reach their ends.
All inputs are finite; a program needn't handle non-finite values.
Results may differ from the reference program's by a relative error of at most 0.015.
Values may be sent and summed in bfloat16 or wider, within the bound.
No kernel may reach another device: no remote copies, remote signals or barrier semaphores. Data moves between devices by JAX's collectives and lax.ppermute only.
A program may use at most 128 MiB of HBM per device.

```python
import math
import jax
import jax.numpy as jnp
from jax import lax

C = 32
NX = 1024
MX = 128
MY = 128
ITERS = 3
LEV = 4
NY = 768


def levels(key, extent, split, least, top_value):
    def one(axis_at, parts):
        draws = jax.random.uniform(jax.random.fold_in(jax.random.fold_in(key, 6), axis_at), (parts,), jnp.float32, least / len(split), top_value / len(split))
        return jnp.repeat(jnp.exp(draws), extent[axis_at] // parts).reshape((-1,) + (1,) * (len(extent) - axis_at - 1))

    level = one(*split[0])
    for cut in split[1:]:
        level = level * one(*cut)
    return level


def normal_values(rng, extent, deviation, most, cuts=(), kind=jnp.bfloat16):
    entries = jax.random.normal(rng, extent, jnp.float32) * deviation
    if len(cuts) > 0:
        entries = levels(rng, extent, cuts, -0.22, 0.18) * entries
    return jnp.clip(entries, min=-most, max=most).astype(kind)


def setup_inputs(seed: int = 0) -> dict:
    key_list = jax.random.split(jax.random.key(seed), 8)
    forcing = normal_values(key_list[0], (LEV, C, NY, NX), 1.0, 6.0, ((0, 4), (2, 8)))
    spectral_weight = normal_values(key_list[1], (2, MX, C, C, MY), 0.7, 4.1875, ((1, 8),))
    point_weight = normal_values(key_list[2], (C, C), C ** -0.5, 1.0)
    point_bias = normal_values(key_list[3], (C,), 0.5, 3.0, (), jnp.float32)
    decoder = normal_values(key_list[4], (4, C), C ** -0.5, 1.0)
    coriolis = jnp.clip(jax.random.uniform(key_list[5], (NY,), jnp.float32, -1.5, 1.5) * levels(key_list[5], (NY,), ((0, 8),), -0.4, 0.0), -1.5, 1.5)
    layer_depth = jnp.clip(jnp.exp(jax.random.uniform(key_list[6], (LEV,), jnp.float32, math.log(0.5), math.log(2.0))), 0.5, 2.0)
    return {"forcing": forcing, "spectral_weight": spectral_weight, "point_weight": point_weight, "point_bias": point_bias, "decoder": decoder, "coriolis": coriolis, "layer_depth": layer_depth}


def angles(row_index, col_index, length):
    phase = (row_index[:, None] * col_index[None, :]) % length
    return phase.astype(jnp.float32) * (2.0 * math.pi / length)


def signed_modes(length, count):
    index = jnp.arange(count, dtype=jnp.int32)
    return jnp.where(index < count // 2, index, index + (length - count)).astype(jnp.int32)


def forward_x(length, count):
    turned = angles(jnp.arange(length, dtype=jnp.int32), jnp.arange(count, dtype=jnp.int32), length)
    return jnp.stack([jnp.cos(turned), -jnp.sin(turned)], 0).astype(jnp.bfloat16)


def forward_y(row_index, length, count):
    turned = angles(row_index, signed_modes(length, count), length)
    cosine = jnp.cos(turned)
    sine = jnp.sin(turned)
    return jnp.stack([jnp.stack([cosine, -sine], 1), jnp.stack([sine, cosine], 1)], 0).astype(jnp.bfloat16)


def inverse_y(row_index, length, count):
    turned = angles(signed_modes(length, count), row_index, length)
    cosine = jnp.cos(turned)
    sine = jnp.sin(turned)
    return jnp.stack([jnp.stack([cosine, sine], 1), jnp.stack([-sine, cosine], 1)], 0).astype(jnp.bfloat16)


def inverse_x(length, count, total):
    index = jnp.arange(count, dtype=jnp.int32)
    turned = angles(index, jnp.arange(length, dtype=jnp.int32), length)
    factor = jnp.where(index == 0, 1.0, 2.0).astype(jnp.float32)[:, None] / total
    return jnp.stack([factor * jnp.cos(turned), -factor * jnp.sin(turned)], 0).astype(jnp.bfloat16)


def mix_modes(spectrum, weights):
    real_part = spectrum[:, :, 0]
    imag_part = spectrum[:, :, 1]
    weight_real = weights[0].astype(jnp.float32)
    weight_imag = weights[1].astype(jnp.float32)
    highest = lax.Precision.HIGHEST
    out_real = jnp.einsum('klim,kiom->klom', real_part, weight_real, precision=highest) - jnp.einsum('klim,kiom->klom', imag_part, weight_imag, precision=highest)
    out_imag = jnp.einsum('klim,kiom->klom', real_part, weight_imag, precision=highest) + jnp.einsum('klim,kiom->klom', imag_part, weight_real, precision=highest)
    return jnp.stack([out_real, out_imag], 2).astype(jnp.bfloat16)


def product(form, left, right):
    return jnp.einsum(form, left.astype(jnp.float32), right.astype(jnp.float32), precision=lax.Precision.HIGHEST)


def shift_diff(field, axis):
    return (jnp.roll(field, -1, axis) - jnp.roll(field, 1, axis)) * 0.5


def reference(forcing, spectral_weight, point_weight, point_bias, decoder, coriolis, layer_depth):
    row_index = jnp.arange(NY, dtype=jnp.int32)
    table_fx = forward_x(NX, MX)
    table_fy = forward_y(row_index, NY, MY)
    table_iy = inverse_y(row_index, NY, MY)
    table_ix = inverse_x(NX, MX, NX * NY)
    offset = point_bias.astype(jnp.float32)[None, :, None, None]

    def level_step(pair):
        current, source = pair
        current = current[None]
        source = source[None]
        near_modes = product('lcyx,rxk->lrcky', current, table_fx).astype(jnp.bfloat16)
        spectrum = product('lrcky,ryqm->klqcm', near_modes, table_fy)
        mixed = mix_modes(spectrum, spectral_weight)
        back_rows = product('klqcm,qmry->lrcky', mixed, table_iy).astype(jnp.bfloat16)
        spread = product('lrcky,rkx->lcyx', back_rows, table_ix)
        pointwise = product('lcyx,co->loyx', current, point_weight)
        updated = jax.nn.gelu(spread + pointwise + offset + source.astype(jnp.float32), approximate=True)
        return updated[0]

    current = forcing
    for iteration in range(ITERS - 1):
        current = lax.map(level_step, (current, forcing)).astype(jnp.bfloat16)
    final_state = lax.map(level_step, (current, forcing))

    def decode_level(level_state):
        return product('cyx,fc->fyx', level_state, decoder)

    fields = lax.map(decode_level, final_state)
    east_wind = fields[:, 0]
    north_wind = fields[:, 1]
    upward = fields[:, 2]
    heat = fields[:, 3]
    geopotential = jnp.cumsum(layer_depth[:, None, None] * heat, axis=0)
    below_level = jnp.concatenate([jnp.zeros_like(upward[:1]), upward[:-1]], 0)
    turning = coriolis[:, None]
    continuity = shift_diff(east_wind, 2) + shift_diff(north_wind, 1) + upward - below_level
    balance_x = turning * north_wind - shift_diff(geopotential, 2)
    balance_y = turning * east_wind + shift_diff(geopotential, 1)
    return final_state, jnp.stack([continuity, balance_x, balance_y], 0)
```

```python
import functools
import math

import jax
import jax.numpy as jnp
import numpy as np
from jax import lax
from jax.experimental import pallas as pl
from jax.experimental.pallas import tpu as pltpu
from jax.sharding import PartitionSpec as P

ITERS = 3
CHUNKS = 2
BF = jnp.bfloat16
F32 = jnp.float32
LANES = 128
PARAMS = dict(vmem_limit_bytes=48 << 20)


def cost(flops, bytes_accessed, transcendentals=0):
    return pl.CostEstimate(
        flops=int(flops), bytes_accessed=int(bytes_accessed), transcendentals=int(transcendentals)
    )


def turned(rows, cols, length):
    phase = (rows[:, None] * cols[None, :]) % length
    return phase.astype(np.float32) * np.float32(2.0 * math.pi / length)


def x_tables(cells, modes, slices, total):
    angle = turned(np.arange(modes, dtype=np.int64), np.arange(cells, dtype=np.int64), cells)
    pair = np.stack([np.cos(angle), -np.sin(angle)], 0).astype(np.float32)
    factor = (np.where(np.arange(modes) == 0, 1.0, 2.0).astype(np.float32) / np.float32(total))
    inverse = pair * factor[None, :, None]
    own = modes // slices

    def by_slice(table):
        table = table.reshape(2, slices, own, cells).transpose(1, 0, 2, 3)
        return table.reshape(slices, 2 * own, cells).astype(BF)

    return by_slice(pair), by_slice(inverse)


def y_table(rows, modes, slices):
    index = np.arange(modes, dtype=np.int64)
    signed = np.where(index < modes // 2, index, index + (rows - modes))
    angle = turned(np.arange(rows, dtype=np.int64), signed, rows)
    both = np.concatenate([np.cos(angle), np.sin(angle)], 1).astype(np.float32)
    return both.reshape(slices, rows // slices, 2 * modes).astype(BF)


def dot(a, b, dims):
    return lax.dot_general(a, b, (dims, ((), ())), preferred_element_type=F32)


def store_near(state, table, near_refs, pack, rows):
    peers = len(near_refs)
    width = LANES // pack
    near = dot(state, table, ((1,), (0,)))
    for d in range(peers):
        parts = [
            near[j * rows : (j + 1) * rows, d * width : (d + 1) * width] for j in range(pack)
        ]
        near_refs[d][0] = jnp.concatenate(parts, 1).astype(BF)


def near_kernel(pack, state_ref, table_ref, *near_refs):
    rows, cells = state_ref.shape[1:]
    state = state_ref[...].reshape(pack * rows, cells)
    store_near(state, table_ref[...], near_refs, pack, rows)


def forward_y_kernel(pack, own, peers, *refs):
    near_refs, table_ref, keep_ref, send_ref = refs[:peers], refs[peers], refs[-2], refs[-1]
    modes = table_ref.shape[1] // 2
    near = jnp.concatenate([ref[0] for ref in near_refs], 0)
    both = dot(near, table_ref[...], ((0,), (0,)))
    for j in range(pack):
        for h, out_ref in ((0, keep_ref), (1, send_ref)):
            at = (j * 2 + h) * 2 * own
            real = both[at : at + own]
            imag = both[at + own : at + 2 * own]
            out_ref[j, :, :modes] = (real[:, :modes] + imag[:, modes:]).astype(out_ref.dtype)
            out_ref[j, :, modes:] = (imag[:, :modes] - real[:, modes:]).astype(out_ref.dtype)


def mix_kernel(chunks, *refs):
    keep_refs, got_refs = refs[:chunks], refs[chunks : 2 * chunks]
    weight_ref, out_ref, spectrum, mixed = refs[2 * chunks :]
    k = pl.program_id(0)
    size = keep_refs[0].shape[0]
    modes = weight_ref.shape[-1]
    outs = weight_ref.shape[3]

    @pl.when(k == 0)
    def _():
        for n in range(chunks):
            spectrum[n * size : (n + 1) * size] = keep_refs[n][...] + got_refs[n][...].astype(F32)

    def step(i, sums):
        real, imag = sums
        value = spectrum[i, pl.ds(k, 1), :]
        s0, s1 = value[:, :modes], value[:, modes:]
        w0 = weight_ref[0, 0, i].astype(F32)
        w1 = weight_ref[1, 0, i].astype(F32)
        return real + (s0 * w0 - s1 * w1), imag + (s0 * w1 + s1 * w0)

    zero = jnp.zeros((outs, modes), F32)
    real, imag = lax.fori_loop(0, size * chunks, step, (zero, zero), unroll=8)
    mixed[k, :, :modes] = real
    mixed[k, :, modes:] = imag

    @pl.when(k == pl.num_programs(0) - 1)
    def _():
        out_ref[...] = jnp.swapaxes(mixed[...], 0, 1).astype(BF)


def inverse_y_kernel(pack, own, peers, mine_ref, theirs_ref, table_ref, *back_refs):
    modes = table_ref.shape[1] // 2
    rows = table_ref.shape[0] // peers
    parts = []
    for j in range(pack):
        for ref in (mine_ref, theirs_ref):
            value = ref[j].astype(F32)
            real, imag = value[:, :modes], value[:, modes:]
            parts.append(jnp.concatenate([real, -imag], 1))
            parts.append(jnp.concatenate([imag, real], 1))
    turned_modes = jnp.concatenate(parts, 0).astype(BF)
    back = dot(table_ref[...], turned_modes, ((1,), (1,)))
    for d in range(peers):
        back_refs[d][0] = back[d * rows : (d + 1) * rows].astype(BF)


def spread_of(pack, back_refs, table_ref):
    width = LANES // pack
    values = [ref[0].astype(F32) for ref in back_refs]
    blocks = [
        jnp.concatenate([v[:, j * width : (j + 1) * width] for v in values], 1).astype(BF)
        for j in range(pack)
    ]
    return dot(jnp.concatenate(blocks, 0), table_ref[...], ((1,), (0,)))


def update_kernel(pack, peers, *refs):
    back_refs, (point_ref, inverse_ref, forward_ref) = refs[:peers], refs[peers : peers + 3]
    state_ref, near_refs = refs[peers + 3], refs[peers + 4 :]
    rows, cells = state_ref.shape[1:]
    point = point_ref[...].reshape(pack * rows, cells)
    updated = jax.nn.gelu(spread_of(pack, back_refs, inverse_ref) + point, approximate=True)
    state = updated.astype(BF)
    state_ref[...] = state.reshape(pack, rows, cells)
    store_near(state, forward_ref[...], near_refs, pack, rows)


def last_kernel(pack, peers, first_group, *refs):
    back_refs = refs[:peers]
    point_ref, inverse_ref, decoder_ref, updated_ref, fields_ref = refs[peers:]
    rows, cells = updated_ref.shape[1:]
    group = pl.program_id(0)
    point = point_ref[...].reshape(pack * rows, cells)
    updated = jax.nn.gelu(spread_of(pack, back_refs, inverse_ref) + point, approximate=True)
    updated_ref[...] = updated.reshape(pack, rows, cells)

    @pl.when(group == 0)
    def _():
        fields_ref[...] = jnp.zeros_like(fields_ref)

    for f in range(fields_ref.shape[0]):
        total = fields_ref[f]
        for j in range(pack):
            weight = decoder_ref[f, (first_group + group) * pack + j]
            total = total + weight * updated[j * rows : (j + 1) * rows]
        fields_ref[f] = total


def pointwise_kernel(chunks, *refs):
    state_refs, (forcing_ref, weight_ref, bias_ref, out_ref) = refs[:chunks], refs[chunks:]
    channels, rows, cells = out_ref.shape
    state = jnp.concatenate([ref[...] for ref in state_refs], 0).reshape(channels * rows, cells)
    source = forcing_ref[...].reshape(channels * rows, cells).astype(F32) + bias_ref[...]
    out = dot(weight_ref[...], state, ((1,), (0,))) + source
    out_ref[...] = out.reshape(channels, rows, cells)


def on_device(forcing, spectral_weight, point_weight, point_bias, decoder, coriolis, layer_depth):
    level_count, channels, rows, cells = forcing.shape
    assert level_count == 1
    forcing = forcing[0]
    slices = lax.axis_size("gy")
    peers = slices // 2
    own = spectral_weight.shape[1]
    modes = own * slices
    ymodes = spectral_weight.shape[4]
    total_rows = rows * slices
    pack = LANES // (4 * own)
    groups = channels // pack
    part = groups // CHUNKS
    size = channels // CHUNKS
    wide = peers * 4 * own
    me = lax.axis_index("gy")

    forward_x, inverse_x = x_tables(cells, modes, slices, cells * total_rows)
    order = jnp.stack([me ^ d ^ (h * peers) for d in range(peers) for h in range(2)])
    near_table = jnp.take(jnp.asarray(forward_x), order, axis=0).reshape(wide, cells).T
    spread_table = jnp.take(jnp.asarray(inverse_x), order, axis=0).reshape(wide, cells)
    row_table = jnp.take(jnp.asarray(y_table(total_rows, ymodes, slices)), order[::2], axis=0)
    row_table = row_table.reshape(peers * rows, 2 * ymodes)

    block = next(b for b in (16, 8, rows) if rows % b == 0)
    square = jnp.kron(point_weight.T.astype(F32), jnp.eye(block, dtype=F32)).astype(BF)
    bias = jnp.repeat(point_bias, block)[:, None]

    def swap(value, distance):
        return lax.ppermute(value, "gy", [(g, g ^ distance) for g in range(slices)])

    def whole(shape):
        return pl.BlockSpec(shape, lambda i: (0,) * len(shape))

    cells_spec = pl.BlockSpec((pack, rows, cells), lambda i: (i, 0, 0))
    lane_spec = pl.BlockSpec((1, rows, LANES), lambda i: (i, 0, 0))
    lane_shape = jax.ShapeDtypeStruct((part, rows, LANES), BF)
    mode_spec = pl.BlockSpec((pack, own, 2 * ymodes), lambda i: (i, 0, 0))
    params = pltpu.CompilerParams(dimension_semantics=("arbitrary",), **PARAMS)
    tile = size * rows * cells

    def offset_spec(n):
        return pl.BlockSpec((pack, rows, cells), lambda i: (i + n * part, 0, 0))

    def near_of(n):
        return pl.pallas_call(
            functools.partial(near_kernel, pack),
            grid=(part,),
            in_specs=[offset_spec(n), whole((cells, wide))],
            out_specs=[lane_spec] * peers,
            out_shape=[lane_shape] * peers,
            compiler_params=params,
            cost_estimate=cost(2 * tile * wide, tile * 2),
            name="near",
        )(forcing, near_table)

    def exchange(parts):
        return [parts[0]] + [swap(parts[d], d) for d in range(1, peers)]

    def forward_y(parts):
        return pl.pallas_call(
            functools.partial(forward_y_kernel, pack, own, peers),
            grid=(part,),
            in_specs=[lane_spec] * peers + [whole(row_table.shape)],
            out_specs=[mode_spec] * 2,
            out_shape=[
                jax.ShapeDtypeStruct((size, own, 2 * ymodes), F32),
                jax.ShapeDtypeStruct((size, own, 2 * ymodes), BF),
            ],
            compiler_params=params,
            cost_estimate=cost(4 * part * LANES * peers * rows * ymodes, 2 * size * rows * wide),
            name="forward_y",
        )(*parts, row_table)

    def mix(kept, got, n):
        mode_whole = whole((size, own, 2 * ymodes))
        return pl.pallas_call(
            functools.partial(mix_kernel, CHUNKS),
            grid=(own,),
            in_specs=[mode_whole] * (2 * CHUNKS)
            + [pl.BlockSpec((2, 1, channels, size, ymodes), lambda k: (0, k, 0, n, 0))],
            out_specs=mode_whole,
            out_shape=jax.ShapeDtypeStruct((size, own, 2 * ymodes), BF),
            scratch_shapes=[
                pltpu.VMEM((channels, own, 2 * ymodes), F32),
                pltpu.VMEM((own, size, 2 * ymodes), F32),
            ],
            compiler_params=params,
            cost_estimate=cost(
                8 * own * channels * size * ymodes, 4 * own * channels * size * ymodes
            ),
            name="mix",
        )(*kept, *got, spectral_weight)

    def inverse_y(mine, theirs):
        return pl.pallas_call(
            functools.partial(inverse_y_kernel, pack, own, peers),
            grid=(part,),
            in_specs=[mode_spec] * 2 + [whole(row_table.shape)],
            out_specs=[lane_spec] * peers,
            out_shape=[lane_shape] * peers,
            compiler_params=params,
            cost_estimate=cost(4 * part * LANES * peers * rows * ymodes, 2 * size * rows * wide),
            name="inverse_y",
        )(mine, theirs, row_table)

    def pointwise(states):
        if len(states) == 1:
            specs = [pl.BlockSpec((channels, block, cells), lambda i: (0, i, 0))]
        else:
            specs = [pl.BlockSpec((size, block, cells), lambda i: (0, i, 0))] * CHUNKS
        return pl.pallas_call(
            functools.partial(pointwise_kernel, len(states)),
            grid=(rows // block,),
            in_specs=specs
            + [
                pl.BlockSpec((channels, block, cells), lambda i: (0, i, 0)),
                whole(square.shape),
                whole(bias.shape),
            ],
            out_specs=pl.BlockSpec((channels, block, cells), lambda i: (0, i, 0)),
            out_shape=jax.ShapeDtypeStruct((channels, rows, cells), F32),
            compiler_params=params,
            cost_estimate=cost(
                2 * channels * block * channels * rows * cells, 8 * channels * rows * cells
            ),
            name="pointwise",
        )(*states, forcing, square, bias)

    def update(backs, point, n):
        out = pl.pallas_call(
            functools.partial(update_kernel, pack, peers),
            grid=(part,),
            in_specs=[lane_spec] * peers
            + [offset_spec(n), whole(spread_table.shape), whole(near_table.shape)],
            out_specs=[cells_spec] + [lane_spec] * peers,
            out_shape=[jax.ShapeDtypeStruct((size, rows, cells), BF)] + [lane_shape] * peers,
            compiler_params=params,
            cost_estimate=cost(4 * tile * wide, 6 * tile, tile),
            name="update",
        )(*backs, point, spread_table, near_table)
        return out[0], out[1:]

    decoder_full = decoder.astype(F32)

    def last(backs, point, n):
        count = decoder.shape[0]
        return pl.pallas_call(
            functools.partial(last_kernel, pack, peers, n * part),
            grid=(part,),
            in_specs=[lane_spec] * peers
            + [
                offset_spec(n),
                whole(spread_table.shape),
                pl.BlockSpec(memory_space=pltpu.SMEM),
            ],
            out_specs=[cells_spec, whole((count, rows, cells))],
            out_shape=[
                jax.ShapeDtypeStruct((size, rows, cells), F32),
                jax.ShapeDtypeStruct((count, rows, cells), F32),
            ],
            compiler_params=params,
            cost_estimate=cost(2 * tile * wide, 8 * tile, tile),
            name="last",
        )(*backs, point, spread_table, decoder_full)

    every = range(CHUNKS)
    nears = [near_of(n) for n in every]
    states = [forcing]
    for iteration in range(ITERS):
        arrived = [exchange(parts) for parts in nears]
        point = pointwise(states)
        halves = [forward_y(parts) for parts in arrived]
        kept = [half[0] for half in halves]
        got = [swap(half[1], peers) for half in halves]
        mixed = [mix(kept, got, n) for n in every]
        theirs = [swap(value, peers) for value in mixed]
        backs = [exchange(inverse_y(mixed[n], theirs[n])) for n in every]
        if iteration < ITERS - 1:
            done = [update(backs[n], point, n) for n in every]
            states = [pair[0] for pair in done]
            nears = [pair[1] for pair in done]
    done = [last(backs[n], point, n) for n in every]
    updated = jnp.concatenate([pair[0] for pair in done], 0)
    east, north, upward, heat = [sum(pair[1][f] for pair in done) for f in range(4)]

    levels = lax.axis_size("lev")
    level = lax.axis_index("lev")

    def from_below(value, step):
        return lax.ppermute(value, "lev", [(s, s + step) for s in range(levels - step)])

    below = from_below(upward, 1)
    geopotential = lax.dynamic_index_in_dim(layer_depth, level, 0, keepdims=False) * heat
    step = 1
    while step < levels:
        geopotential = geopotential + from_below(geopotential, step)
        step *= 2

    up = [(i, (i + 1) % slices) for i in range(slices)]
    down = [(j, i) for i, j in up]
    pair = jnp.stack([north, geopotential], 0)
    before = lax.ppermute(pair[:, -1:], "gy", up)
    after = lax.ppermute(pair[:, :1], "gy", down)
    rimmed = jnp.concatenate([before, pair, after], 1)
    along_y = (rimmed[:, 2:] - rimmed[:, :-2]) * 0.5

    def along_x(field):
        return (jnp.roll(field, -1, 1) - jnp.roll(field, 1, 1)) * 0.5

    turning = coriolis[:, None]
    continuity = along_x(east) + along_y[0] + upward - below
    balance_x = turning * north - along_x(geopotential)
    balance_y = turning * east + along_y[1]
    return updated[None], jnp.stack([continuity, balance_x, balance_y], 0)[:, None]


def solution(mesh):
    return jax.shard_map(
        on_device,
        mesh=mesh,
        in_specs=(
            P("lev", None, "gy", None),
            P(None, "gy", None, None, None),
            P(),
            P(),
            P(),
            P("gy"),
            P(),
        ),
        out_specs=(P("lev", None, "gy", None), P(None, "lev", "gy", None)),
        check_vma=False,
    )
```

```python
import functools
import math

import jax
import jax.numpy as jnp
import numpy as np
from jax import lax
from jax.experimental import pallas as pl
from jax.experimental.pallas import tpu as pltpu
from jax.sharding import PartitionSpec as P

ITERS = 3
CHUNKS = 2
BF = jnp.bfloat16
F32 = jnp.float32
LANES = 128


def cost(flops, bytes_accessed, transcendentals=0):
    return pl.CostEstimate(
        flops=int(flops), bytes_accessed=int(bytes_accessed), transcendentals=int(transcendentals)
    )


def turned(rows, cols, length):
    phase = (rows[:, None] * cols[None, :]) % length
    return phase.astype(np.float32) * np.float32(2.0 * math.pi / length)


def x_tables(cells, modes, slices, total):
    angle = turned(np.arange(modes, dtype=np.int64), np.arange(cells, dtype=np.int64), cells)
    pair = np.stack([np.cos(angle), -np.sin(angle)], 0).astype(np.float32)
    factor = (np.where(np.arange(modes) == 0, 1.0, 2.0).astype(np.float32) / np.float32(total))
    inverse = pair * factor[None, :, None]
    own = modes // slices

    def by_slice(table):
        table = table.reshape(2, slices, own, cells).transpose(1, 0, 2, 3)
        return table.reshape(slices, 2 * own, cells).astype(BF)

    return by_slice(pair), by_slice(inverse)


def y_table(rows, modes, slices):
    index = np.arange(modes, dtype=np.int64)
    signed = np.where(index < modes // 2, index, index + (rows - modes))
    angle = turned(np.arange(rows, dtype=np.int64), signed, rows)
    both = np.concatenate([np.cos(angle), np.sin(angle)], 1).astype(np.float32)
    return both.reshape(slices, rows // slices, 2 * modes).astype(BF)


def dot(a, b, dims):
    return lax.dot_general(a, b, (dims, ((), ())), preferred_element_type=F32)


def store_near(state, table, near_refs, pack, rows, first=0):
    width = LANES // pack
    near = dot(state, table, ((1,), (0,)))
    for g in range(state.shape[0] // (pack * rows)):
        for d, ref in enumerate(near_refs):
            parts = []
            for j in range(pack):
                at = (g * pack + j) * rows
                parts.append(near[at : at + rows, d * width : (d + 1) * width])
            ref[first + g] = jnp.concatenate(parts, 1).astype(BF)


def near_kernel(pack, state_ref, table_ref, *near_refs):
    count, rows, cells = state_ref.shape
    state = state_ref[...].reshape(count * rows, cells)
    store_near(state, table_ref[...], near_refs, pack, rows)


def forward_y_kernel(pack, own, peers, *refs):
    near_refs, table_ref, keep_ref, send_ref = refs[:peers], refs[peers], refs[-2], refs[-1]
    modes = table_ref.shape[1] // 2
    for g in range(near_refs[0].shape[0]):
        near = jnp.concatenate([ref[g] for ref in near_refs], 0)
        both = dot(near, table_ref[...], ((0,), (0,)))
        for j in range(pack):
            for h, out_ref in ((0, keep_ref), (1, send_ref)):
                at = (j * 2 + h) * 2 * own
                real = both[at : at + own]
                imag = both[at + own : at + 2 * own]
                c = g * pack + j
                out_ref[c, :, :modes] = (real[:, :modes] + imag[:, modes:]).astype(out_ref.dtype)
                out_ref[c, :, modes:] = (imag[:, :modes] - real[:, modes:]).astype(out_ref.dtype)


def mix_kernel(chunks, *refs):
    keep_refs, got_refs = refs[:chunks], refs[chunks : 2 * chunks]
    weight_ref = refs[2 * chunks]
    out_refs = refs[2 * chunks + 1 : 3 * chunks + 1]
    spectrum, mixed = refs[3 * chunks + 1 :]
    own, channels, modes = weight_ref.shape[1], weight_ref.shape[2], weight_ref.shape[4]
    size = channels // chunks
    for n in range(chunks):
        value = keep_refs[n][...] + got_refs[n][...].astype(F32)
        spectrum[:, n * size : (n + 1) * size] = jnp.swapaxes(value, 0, 1)

    def step(k, carry):
        row = spectrum[k]
        real = [jnp.zeros((channels, modes), F32)] * 2
        imag = [jnp.zeros((channels, modes), F32)] * 2
        for i in range(channels):
            s0, s1 = row[i : i + 1, :modes], row[i : i + 1, modes:]
            w0 = weight_ref[0, k, i].astype(F32)
            w1 = weight_ref[1, k, i].astype(F32)
            real[i % 2] = real[i % 2] + (s0 * w0 - s1 * w1)
            imag[i % 2] = imag[i % 2] + (s0 * w1 + s1 * w0)
        mixed[k, :, :modes] = real[0] + real[1]
        mixed[k, :, modes:] = imag[0] + imag[1]
        return carry

    lax.fori_loop(0, own, step, 0)
    for n in range(chunks):
        value = jnp.swapaxes(mixed[:, n * size : (n + 1) * size], 0, 1)
        out_refs[n][...] = value.astype(BF)


def inverse_y_kernel(pack, own, peers, mine_ref, theirs_ref, table_ref, *back_refs):
    modes = table_ref.shape[1] // 2
    rows = table_ref.shape[0] // peers
    for g in range(back_refs[0].shape[0]):
        parts = []
        for j in range(pack):
            for ref in (mine_ref, theirs_ref):
                value = ref[g * pack + j].astype(F32)
                real, imag = value[:, :modes], value[:, modes:]
                parts.append(jnp.concatenate([real, -imag], 1))
                parts.append(jnp.concatenate([imag, real], 1))
        turned_modes = jnp.concatenate(parts, 0).astype(BF)
        back = dot(table_ref[...], turned_modes, ((1,), (1,)))
        for d in range(peers):
            back_refs[d][g] = back[d * rows : (d + 1) * rows].astype(BF)


def spread_of(pack, back_refs, table_ref):
    width = LANES // pack
    blocks = []
    for g in range(back_refs[0].shape[0]):
        values = [ref[g].astype(F32) for ref in back_refs]
        for j in range(pack):
            lanes = [v[:, j * width : (j + 1) * width] for v in values]
            blocks.append(jnp.concatenate(lanes, 1).astype(BF))
    return dot(jnp.concatenate(blocks, 0), table_ref[...], ((1,), (0,)))


def update_kernel(pack, peers, *refs):
    back_refs, (point_ref, inverse_ref, forward_ref) = refs[:peers], refs[peers : peers + 3]
    state_ref, near_refs = refs[peers + 3], refs[peers + 4 :]
    count, rows, cells = state_ref.shape
    point = point_ref[...].reshape(count * rows, cells)
    updated = jax.nn.gelu(spread_of(pack, back_refs, inverse_ref) + point, approximate=True)
    state = updated.astype(BF)
    state_ref[...] = state.reshape(count, rows, cells)
    store_near(state, forward_ref[...], near_refs, pack, rows)


def last_kernel(pack, peers, first, *refs):
    back_refs = refs[:peers]
    point_ref, inverse_ref, decoder_ref = refs[peers : peers + 3]
    earlier = refs[peers + 3 : -2]
    updated_ref, fields_ref = refs[-2:]
    count, rows, cells = updated_ref.shape
    group = pl.program_id(0)
    point = point_ref[...].reshape(count * rows, cells)
    updated = jax.nn.gelu(spread_of(pack, back_refs, inverse_ref) + point, approximate=True)
    updated_ref[...] = updated.reshape(count, rows, cells)

    @pl.when(group == 0)
    def _():
        fields_ref[...] = earlier[1][...] if earlier else jnp.zeros_like(fields_ref)

    def slab(t, carry):
        at = pl.ds(pl.multiple_of(t * 8, 8), 8)
        values = [updated_ref[c, at, :] for c in range(count)]
        for f in range(fields_ref.shape[0]):
            total = fields_ref[f, at, :]
            for c in range(count):
                total = total + decoder_ref[f, first + group * count + c] * values[c]
            fields_ref[f, at, :] = total
        return carry

    lax.fori_loop(0, rows // 8, slab, 0)


def pointwise_kernel(chunks, block, *refs):
    state_refs, (forcing_ref, weight_ref, bias_ref, out_ref) = refs[:chunks], refs[chunks:]
    channels, rows, cells = out_ref.shape
    count = channels * block
    for t in range(rows // block):
        at = slice(t * block, (t + 1) * block)
        state = jnp.concatenate([ref[:, at] for ref in state_refs], 0).reshape(count, cells)
        source = forcing_ref[:, at].reshape(count, cells).astype(F32) + bias_ref[...]
        out = dot(weight_ref[...], state, ((1,), (0,))) + source
        out_ref[:, at] = out.reshape(channels, block, cells)


def residual_kernel(
    fields_ref, geo_ref, below_ref, before_ref, after_ref, turning_ref, out_ref
):
    rows, cells = geo_ref.shape
    east, north, upward = fields_ref[0], fields_ref[1], fields_ref[2]
    geopotential = geo_ref[...]
    row = lax.broadcasted_iota(jnp.int32, (rows, cells), 0)

    def along_x(field):
        return (pltpu.roll(field, cells - 1, 1) - pltpu.roll(field, 1, 1)) * 0.5

    def along_y(field, which):
        later = jnp.where(row == rows - 1, after_ref[which], pltpu.roll(field, rows - 1, 0))
        earlier = jnp.where(row == 0, before_ref[which], pltpu.roll(field, 1, 0))
        return (later - earlier) * 0.5

    turning = turning_ref[...]
    out_ref[0] = along_x(east) + along_y(north, 0) + upward - below_ref[...]
    out_ref[1] = turning * north - along_x(geopotential)
    out_ref[2] = turning * east + along_y(geopotential, 1)


def on_device(forcing, spectral_weight, point_weight, point_bias, decoder, coriolis, layer_depth):
    level_count, channels, rows, cells = forcing.shape
    assert level_count == 1
    forcing = forcing[0]
    slices = lax.axis_size("gy")
    peers = slices // 2
    own = spectral_weight.shape[1]
    modes = own * slices
    ymodes = spectral_weight.shape[4]
    total_rows = rows * slices
    pack = LANES // (4 * own)
    groups = channels // pack
    part = groups // CHUNKS
    size = channels // CHUNKS
    wide = peers * 4 * own
    me = lax.axis_index("gy")

    forward_x, inverse_x = x_tables(cells, modes, slices, cells * total_rows)
    order = jnp.stack([me ^ d ^ (h * peers) for d in range(peers) for h in range(2)])
    near_table = jnp.take(jnp.asarray(forward_x), order, axis=0).reshape(wide, cells).T
    spread_table = jnp.take(jnp.asarray(inverse_x), order, axis=0).reshape(wide, cells)
    row_table = jnp.take(jnp.asarray(y_table(total_rows, ymodes, slices)), order[::2], axis=0)
    row_table = row_table.reshape(peers * rows, 2 * ymodes)

    block = next(b for b in (16, 8, rows) if rows % b == 0)
    blocks = next(b for b in (2, 1) if rows % (b * block) == 0)
    which = lax.broadcasted_iota(jnp.int32, (channels * block, channels), 0) // block
    pick = (which == lax.broadcasted_iota(jnp.int32, which.shape, 1)).astype(BF)
    square = jnp.dot(jnp.dot(pick, point_weight.T), pick.T)
    at = jnp.arange(channels * block, dtype=jnp.int32) % block
    square = jnp.where(at[:, None] == at[None, :], square, 0).astype(BF)
    bias = jnp.repeat(point_bias, block)[:, None]
    many = next(b for b in (4, 2, 1) if part % b == 0)

    def swap(value, distance):
        return lax.ppermute(value, "gy", [(g, g ^ distance) for g in range(slices)])

    def whole(shape):
        return pl.BlockSpec(shape, lambda i: (0,) * len(shape))

    cells_spec = pl.BlockSpec((many * pack, rows, cells), lambda i: (i, 0, 0))
    lane_spec = pl.BlockSpec((many, rows, LANES), lambda i: (i, 0, 0))
    lane_shape = jax.ShapeDtypeStruct((part, rows, LANES), BF)
    mode_spec = pl.BlockSpec((many * pack, own, 2 * ymodes), lambda i: (i, 0, 0))
    vmem = pl.BlockSpec(memory_space=pltpu.VMEM)

    def params(mib, *grid):
        return pltpu.CompilerParams(dimension_semantics=grid, vmem_limit_bytes=mib << 20)

    tile = size * rows * cells

    def offset_spec(n):
        return pl.BlockSpec((many * pack, rows, cells), lambda i: (i + n * (part // many), 0, 0))

    def near_of(n):
        return pl.pallas_call(
            functools.partial(near_kernel, pack),
            grid=(part // many,),
            in_specs=[offset_spec(n), whole((cells, wide))],
            out_specs=[lane_spec] * peers,
            out_shape=[lane_shape] * peers,
            compiler_params=params(6, "arbitrary"),
            cost_estimate=cost(2 * tile * wide, tile * 2),
            name="near",
        )(forcing, near_table)

    def exchange(parts):
        return [parts[0]] + [swap(parts[d], d) for d in range(1, peers)]

    def forward_y(parts):
        return pl.pallas_call(
            functools.partial(forward_y_kernel, pack, own, peers),
            grid=(part // many,),
            in_specs=[lane_spec] * peers + [whole(row_table.shape)],
            out_specs=[mode_spec] * 2,
            out_shape=[
                jax.ShapeDtypeStruct((size, own, 2 * ymodes), F32),
                jax.ShapeDtypeStruct((size, own, 2 * ymodes), BF),
            ],
            compiler_params=params(8, "arbitrary"),
            cost_estimate=cost(4 * part * LANES * peers * rows * ymodes, 2 * size * rows * wide),
            name="forward_y",
        )(*parts, row_table)

    def mix(kept, got):
        return pl.pallas_call(
            functools.partial(mix_kernel, CHUNKS),
            in_specs=[vmem] * (2 * CHUNKS + 1),
            out_specs=[vmem] * CHUNKS,
            out_shape=[jax.ShapeDtypeStruct((size, own, 2 * ymodes), BF)] * CHUNKS,
            scratch_shapes=[pltpu.VMEM((own, channels, 2 * ymodes), F32)] * 2,
            compiler_params=params(8),
            cost_estimate=cost(
                8 * own * channels**2 * ymodes, 4 * own * channels**2 * ymodes
            ),
            name="mix",
        )(*kept, *got, spectral_weight)

    def inverse_y(mine, theirs):
        return pl.pallas_call(
            functools.partial(inverse_y_kernel, pack, own, peers),
            grid=(part // many,),
            in_specs=[mode_spec] * 2 + [whole(row_table.shape)],
            out_specs=[lane_spec] * peers,
            out_shape=[lane_shape] * peers,
            compiler_params=params(8, "arbitrary"),
            cost_estimate=cost(4 * part * LANES * peers * rows * ymodes, 2 * size * rows * wide),
            name="inverse_y",
        )(mine, theirs, row_table)

    def pointwise(states):
        if len(states) == 1:
            specs = [pl.BlockSpec((channels, blocks * block, cells), lambda i: (0, i, 0))]
        else:
            specs = [pl.BlockSpec((size, blocks * block, cells), lambda i: (0, i, 0))] * CHUNKS
        return pl.pallas_call(
            functools.partial(pointwise_kernel, len(states), block),
            grid=(rows // (blocks * block),),
            in_specs=specs
            + [
                pl.BlockSpec((channels, blocks * block, cells), lambda i: (0, i, 0)),
                whole(square.shape),
                whole(bias.shape),
            ],
            out_specs=pl.BlockSpec((channels, blocks * block, cells), lambda i: (0, i, 0)),
            out_shape=jax.ShapeDtypeStruct((channels, rows, cells), F32),
            compiler_params=params(19, "arbitrary"),
            cost_estimate=cost(
                2 * channels * block * channels * rows * cells, 8 * channels * rows * cells
            ),
            name="pointwise",
        )(*states, forcing, square, bias)

    def update(backs, point, n):
        out = pl.pallas_call(
            functools.partial(update_kernel, pack, peers),
            grid=(part // many,),
            in_specs=[lane_spec] * peers
            + [offset_spec(n), whole(spread_table.shape), whole(near_table.shape)],
            out_specs=[cells_spec] + [lane_spec] * peers,
            out_shape=[jax.ShapeDtypeStruct((size, rows, cells), BF)] + [lane_shape] * peers,
            compiler_params=params(16, "arbitrary"),
            cost_estimate=cost(4 * tile * wide, 6 * tile, tile),
            name="update",
        )(*backs, point, spread_table, near_table)
        return out[0], out[1:]

    decoder_full = decoder.astype(F32)

    def last(backs, point, n, earlier):
        fields_shape = (decoder.shape[0], rows, cells)
        more = [pl.BlockSpec(memory_space=pl.ANY), whole(fields_shape)] if earlier else []
        return pl.pallas_call(
            functools.partial(last_kernel, pack, peers, n * size),
            grid=(part // many,),
            in_specs=[lane_spec] * peers
            + [
                offset_spec(n),
                whole(spread_table.shape),
                pl.BlockSpec(memory_space=pltpu.SMEM),
            ]
            + more,
            out_specs=[offset_spec(n), whole(fields_shape)],
            out_shape=[
                jax.ShapeDtypeStruct((channels, rows, cells), F32),
                jax.ShapeDtypeStruct(fields_shape, F32),
            ],
            input_output_aliases={peers + 3: 0} if earlier else {},
            compiler_params=params(20, "arbitrary"),
            cost_estimate=cost(2 * tile * wide, 8 * tile, tile),
            name="last",
        )(*backs, point, spread_table, decoder_full, *earlier)

    every = range(CHUNKS)
    nears = [near_of(n) for n in every]
    states = [forcing]
    for iteration in range(ITERS):
        arrived = [exchange(parts) for parts in nears]
        point = pointwise(states)
        halves = [forward_y(parts) for parts in arrived]
        kept = [half[0] for half in halves]
        got = [swap(half[1], peers) for half in halves]
        mixed = mix(kept, got)
        theirs = [swap(value, peers) for value in mixed]
        backs = [exchange(inverse_y(mixed[n], theirs[n])) for n in every]
        if iteration < ITERS - 1:
            done = [update(backs[n], point, n) for n in every]
            states = [pair[0] for pair in done]
            nears = [pair[1] for pair in done]
    done = []
    for n in every:
        done = last(backs[n], point, n, done)
    updated, fields = done
    north, upward, heat = fields[1], fields[2], fields[3]

    levels = lax.axis_size("lev")
    level = lax.axis_index("lev")

    def from_below(value, step):
        return lax.ppermute(value, "lev", [(s, s + step) for s in range(levels - step)])

    below = from_below(upward, 1)
    layer = lax.dynamic_index_in_dim(layer_depth, level, 0, keepdims=False) * heat
    if levels % 2 == 0 and rows % 16 == 0:
        half = rows // 2
        place = level % 2
        partner = [(s, s ^ 1) for s in range(levels)]
        other = lax.ppermute(layer, "lev", partner)
        both = lax.dynamic_slice_in_dim(layer + other, place * half, half, 0)
        lower = from_below(both, 2)
        step = 2
        while step < levels - 2:
            lower = lower + from_below(lower, step)
            step *= 2
        rest = lax.ppermute(lower, "lev", partner)
        lower = jnp.where(
            place == 0, jnp.concatenate([lower, rest], 0), jnp.concatenate([rest, lower], 0)
        )
        geopotential = layer + jnp.where(place == 0, 0.0, other) + lower
    else:
        geopotential = layer
        step = 1
        while step < levels:
            geopotential = geopotential + from_below(geopotential, step)
            step *= 2

    up = [(i, (i + 1) % slices) for i in range(slices)]
    down = [(j, i) for i, j in up]
    before = lax.ppermute(jnp.stack([north[-1:], geopotential[-1:]], 0), "gy", up)
    after = lax.ppermute(jnp.stack([north[:1], geopotential[:1]], 0), "gy", down)
    residual = pl.pallas_call(
        residual_kernel,
        in_specs=[vmem] * 6,
        out_specs=vmem,
        out_shape=jax.ShapeDtypeStruct((3, rows, cells), F32),
        compiler_params=params(8),
        cost_estimate=cost(20 * rows * cells, 36 * rows * cells),
        name="residual",
    )(fields, geopotential, below, before, after, coriolis[:, None])
    return updated[None], residual[:, None]


def solution(mesh):
    return jax.shard_map(
        on_device,
        mesh=mesh,
        in_specs=(
            P("lev", None, "gy", None),
            P(None, "gy", None, None, None),
            P(),
            P(),
            P(),
            P("gy"),
            P(),
        ),
        out_specs=(P("lev", None, "gy", None), P(None, "lev", "gy", None)),
        check_vma=False,
    )
```

```python
import functools
import math

import jax
import jax.numpy as jnp
import numpy as np
from jax import lax
from jax.experimental import pallas as pl
from jax.experimental.pallas import tpu as pltpu
from jax.sharding import PartitionSpec as P


ITERS = 3
CHUNKS = 2
BF = jnp.bfloat16
F32 = jnp.float32
LANES = 128


def cost(flops, bytes_accessed, transcendentals=0):
    return pl.CostEstimate(
        flops=int(flops), bytes_accessed=int(bytes_accessed), transcendentals=int(transcendentals)
    )


def turned(rows, cols, length):
    phase = (rows[:, None] * cols[None, :]) % length
    return phase.astype(np.float32) * np.float32(2.0 * math.pi / length)


def x_tables(cells, modes, slices, total):
    angle = turned(np.arange(modes, dtype=np.int64), np.arange(cells, dtype=np.int64), cells)
    pair = np.stack([np.cos(angle), -np.sin(angle)], 0).astype(np.float32)
    factor = (np.where(np.arange(modes) == 0, 1.0, 2.0).astype(np.float32) / np.float32(total))
    inverse = pair * factor[None, :, None]
    own = modes // slices

    def by_slice(table):
        table = table.reshape(2, slices, own, cells).transpose(1, 0, 2, 3)
        return table.reshape(slices, 2 * own, cells).astype(BF)

    order = [d + h * (slices // 2) for d in range(slices // 2) for h in range(2)]
    first, second = [by_slice(table)[order].reshape(-1, cells) for table in (pair, inverse)]
    return np.ascontiguousarray(first.T), second


def y_table(rows, modes, slices):
    index = np.arange(modes, dtype=np.int64)
    signed = np.where(index < modes // 2, index, index + (rows - modes))
    angle = turned(np.arange(rows, dtype=np.int64), signed, rows)
    both = np.concatenate([np.cos(angle), np.sin(angle)], 1).astype(np.float32)
    return both.reshape(slices, rows // slices, 2 * modes).astype(BF)


def dot(a, b, dims):
    return lax.dot_general(a, b, (dims, ((), ())), preferred_element_type=F32)


def store_near(state, table, near_refs, pack, rows, first=0):
    width = LANES // pack
    near = dot(state, table, ((1,), (0,)))
    for g in range(state.shape[0] // (pack * rows)):
        for d, ref in enumerate(near_refs):
            parts = []
            for j in range(pack):
                at = (g * pack + j) * rows
                parts.append(near[at : at + rows, d * width : (d + 1) * width])
            ref[first + g] = jnp.concatenate(parts, 1).astype(BF)


def near_kernel(pack, state_ref, table_ref, *near_refs):
    count, rows, cells = state_ref.shape
    state = state_ref[...].reshape(count * rows, cells)
    store_near(state, table_ref[...], near_refs, pack, rows)


def slice_order(own, peers, me, across, along):
    wide = peers * 4 * own
    block = 2 * own
    mask = ((me % peers) * 2) | (me // peers)
    place = lax.broadcasted_iota(jnp.int32, (wide, wide), across)
    source = ((place // block) ^ mask) * block + place % block
    return (lax.broadcasted_iota(jnp.int32, (wide, wide), along) == source).astype(BF)


def forward_table_kernel(own, peers, me_ref, forward_ref, near_ref):
    order = slice_order(own, peers, me_ref[0], 1, 0)
    near_ref[...] = dot(forward_ref[...], order, ((1,), (0,))).astype(BF)


def other_tables_kernel(own, peers, me_ref, inverse_ref, row_ref, spread_ref, rows_ref):
    order = slice_order(own, peers, me_ref[0], 0, 1)
    spread_ref[...] = dot(order, inverse_ref[...], ((1,), (0,))).astype(BF)
    rows = row_ref.shape[1]
    for d in range(peers):
        rows_ref[d * rows : (d + 1) * rows] = row_ref[me_ref[0] ^ d]


def small_kernel(block, weight_ref, bias_ref, decoder_ref, square_ref, column_ref, splat_ref):
    channels = weight_ref.shape[0]
    count = channels * block
    row = lax.broadcasted_iota(jnp.int32, (count, channels), 0) // block
    mine = row == lax.broadcasted_iota(jnp.int32, (count, channels), 1)
    pick = mine.astype(BF)
    left = dot(pick, weight_ref[...], ((1,), (1,))).astype(BF)
    full = dot(left, pick, ((1,), (1,)))
    down = lax.broadcasted_iota(jnp.int32, (count, count), 0) % block
    across = lax.broadcasted_iota(jnp.int32, (count, count), 1) % block
    square_ref[...] = jnp.where(down == across, full, 0.0).astype(BF)
    column_ref[...] = jnp.sum(jnp.where(mine, bias_ref[...], 0.0), 1, keepdims=True)
    fields = decoder_ref.shape[0]
    lines = channels * fields
    row = lax.broadcasted_iota(jnp.int32, (lines, channels), 0) // fields
    pick = (row == lax.broadcasted_iota(jnp.int32, (lines, channels), 1)).astype(BF)
    values = dot(pick, decoder_ref[...], ((1,), (1,)))
    row = lax.broadcasted_iota(jnp.int32, (lines, fields), 0) % fields
    own = row == lax.broadcasted_iota(jnp.int32, (lines, fields), 1)
    value = jnp.sum(jnp.where(own, values, 0.0), 1, keepdims=True)
    splat_ref[...] = jnp.broadcast_to(value, splat_ref.shape)


def forward_y_kernel(pack, own, peers, *refs):
    near_refs, (table_ref, keep_ref, send_ref) = refs[:peers], refs[peers:]
    modes = table_ref.shape[1] // 2
    for g in range(near_refs[0].shape[0]):
        near = jnp.concatenate([ref[g] for ref in near_refs], 0)
        both = dot(near, table_ref[...], ((0,), (0,)))
        for j in range(pack):
            for h, out_ref in ((0, keep_ref), (1, send_ref)):
                at = (j * 2 + h) * 2 * own
                real = both[at : at + own]
                imag = both[at + own : at + 2 * own]
                c = g * pack + j
                out_ref[c, :, :modes] = (real[:, :modes] + imag[:, modes:]).astype(out_ref.dtype)
                out_ref[c, :, modes:] = (imag[:, :modes] - real[:, modes:]).astype(out_ref.dtype)


def mix_kernel(n, chunks, *refs):
    keep_ref, got_ref, weight_ref = refs[:3]
    earlier = refs[3:4] if n > 0 else ()
    out_refs = refs[3 + len(earlier) : -1]
    spectrum = refs[-1]
    own, channels, modes = weight_ref.shape[1], weight_ref.shape[2], weight_ref.shape[4]
    size = channels // chunks
    value = keep_ref[...] + got_ref[...].astype(F32)
    spectrum[...] = jnp.swapaxes(value, 0, 1)
    total = out_refs[0] if n < chunks - 1 else earlier[0]

    def step(k, carry):
        row = spectrum[k]
        zero = jnp.zeros((channels, modes), F32)
        real, imag = [zero, zero], [zero, zero]
        if earlier:
            real[0], imag[0] = earlier[0][k, :, :modes], earlier[0][k, :, modes:]
        for i in range(size):
            s0, s1 = row[i : i + 1, :modes], row[i : i + 1, modes:]
            w0 = weight_ref[0, k, n * size + i].astype(F32)
            w1 = weight_ref[1, k, n * size + i].astype(F32)
            real[i % 2] = real[i % 2] + (s0 * w0 - s1 * w1)
            imag[i % 2] = imag[i % 2] + (s0 * w1 + s1 * w0)
        total[k, :, :modes] = real[0] + real[1]
        total[k, :, modes:] = imag[0] + imag[1]
        return carry

    lax.fori_loop(0, own, step, 0)
    if n == chunks - 1:
        for c in range(chunks):
            part = jnp.swapaxes(total[:, c * size : (c + 1) * size], 0, 1)
            out_refs[c][...] = part.astype(BF)


def inverse_y_kernel(pack, peers, mine_ref, theirs_ref, table_ref, *back_refs):
    rows, modes = table_ref.shape[0] // peers, table_ref.shape[1] // 2
    for g in range(back_refs[0].shape[0]):
        parts = []
        for j in range(pack):
            for ref in (mine_ref, theirs_ref):
                value = ref[g * pack + j].astype(F32)
                real, imag = value[:, :modes], value[:, modes:]
                parts.append(jnp.concatenate([real, -imag], 1))
                parts.append(jnp.concatenate([imag, real], 1))
        turned_modes = jnp.concatenate(parts, 0).astype(BF)
        back = dot(table_ref[...], turned_modes, ((1,), (1,)))
        for d in range(peers):
            back_refs[d][g] = back[d * rows : (d + 1) * rows].astype(BF)


def spread_of(pack, back_refs, table_ref):
    width = LANES // pack
    blocks = []
    for g in range(back_refs[0].shape[0]):
        values = [ref[g].astype(F32) for ref in back_refs]
        for j in range(pack):
            lanes = [v[:, j * width : (j + 1) * width] for v in values]
            blocks.append(jnp.concatenate(lanes, 1).astype(BF))
    return dot(jnp.concatenate(blocks, 0), table_ref[...], ((1,), (0,)))


def update_kernel(pack, peers, *refs):
    back_refs, (point_ref, inverse_ref, forward_ref) = refs[:peers], refs[peers : peers + 3]
    state_ref, near_refs = refs[peers + 3], refs[peers + 4 :]
    count, rows, cells = state_ref.shape
    point = point_ref[...].reshape(count * rows, cells)
    updated = jax.nn.gelu(spread_of(pack, back_refs, inverse_ref) + point, approximate=True)
    state = updated.astype(BF)
    state_ref[...] = state.reshape(count, rows, cells)
    store_near(state, forward_ref[...], near_refs, pack, rows)


def last_kernel(pack, peers, first, kinds, *refs):
    back_refs = refs[:peers]
    me_ref, depth_ref, point_ref, inverse_ref, decoder_ref = refs[peers : peers + 5]
    updated_ref, *field_refs = refs[-kinds - 3 : -2]
    earlier = refs[peers + 5 : -kinds - 3]
    low_ref, high_ref = refs[-2:]
    count, rows, cells = updated_ref.shape
    group = pl.program_id(0)
    point = point_ref[...].reshape(count * rows, cells)
    updated = jax.nn.gelu(spread_of(pack, back_refs, inverse_ref) + point, approximate=True)
    updated_ref[...] = updated.reshape(count, rows, cells)

    @pl.when(group == 0)
    def _():
        for f in range(kinds):
            field_refs[f][...] = (
                earlier[1 + f][...] if earlier else jnp.zeros((rows, cells), F32)
            )

    lanes = next(b for b in (LANES, cells) if cells % b == 0)
    depth = depth_ref[me_ref[1]]
    weights = []
    for f in range(kinds):
        lines = [
            decoder_ref[pl.ds((first + group * count + c) * kinds + f, 1), :]
            for c in range(count)
        ]
        lines = [line * depth for line in lines] if f == kinds - 1 else lines
        weights.append([jnp.broadcast_to(line, (8, lanes)) for line in lines])

    def slab(t, carry):
        at = pl.ds(pl.multiple_of(t * 8, 8), 8)
        for start in range(0, cells, lanes):
            to = slice(start, start + lanes)
            values = [updated_ref[c, at, to] for c in range(count)]
            for f in range(kinds):
                terms = [weights[f][c] * values[c] for c in range(count)]
                while len(terms) > 1:
                    terms = [sum(terms[i + 1 : i + 2], terms[i]) for i in range(0, len(terms), 2)]
                field_refs[f][at, to] += terms[0]
        return carry

    lax.fori_loop(0, rows // 8, slab, 0)

    @pl.when(group == pl.num_programs(0) - 1)
    def _():
        for i, f in enumerate((1, kinds - 1)):
            low_ref[i : i + 1] = field_refs[f][:1]
            high_ref[i : i + 1] = field_refs[f][rows - 1 :]


def pair_kernel(me_ref, layer_ref, other_ref, both_ref):
    half = both_ref.shape[0]
    at = pl.ds(pl.multiple_of((me_ref[1] & 1) * half, 8), half)
    both_ref[...] = layer_ref[at, :] + other_ref[at, :]


def pointwise_kernel(chunks, block, *refs):
    state_refs, (forcing_ref, weight_ref, bias_ref, out_ref) = refs[:chunks], refs[chunks:]
    channels, rows, cells = out_ref.shape
    count = channels * block
    for t in range(rows // block):
        at = slice(t * block, (t + 1) * block)
        state = jnp.concatenate([ref[:, at] for ref in state_refs], 0).reshape(count, cells)
        source = forcing_ref[:, at].reshape(count, cells).astype(F32) + bias_ref[...]
        out = dot(weight_ref[...], state, ((1,), (0,))) + source
        out_ref[:, at] = out.reshape(channels, block, cells)


def residual_kernel(paired, shifts, *refs):
    east_ref, north_ref, upward_ref, layer_ref, below_ref, before_ref, after_ref = refs[:7]
    shift_refs, rest, out_ref = refs[7 : 7 + shifts], refs[7 + shifts : -1], refs[-1]
    rows, cells = layer_ref.shape
    geopotential = layer_ref[...]
    turning_ref, lower_refs = rest[0], rest[1:]
    if paired:
        me_ref, other_ref, mine_ref, partner_ref = lower_refs
        odd = (me_ref[1] & 1) == 1
        mine, theirs = mine_ref[...], partner_ref[...]
        lower = jnp.concatenate(
            [jnp.where(odd, theirs, mine), jnp.where(odd, mine, theirs)], 0
        )
        geopotential = geopotential + jnp.where(odd, other_ref[...], 0.0) + lower
    else:
        for ref in lower_refs:
            geopotential = geopotential + ref[...]
    rims = [before_ref[1:2], after_ref[1:2]]
    for ref in shift_refs:
        rims = [rims[0] + ref[:1], rims[1] + ref[1:2]]
    row = lax.broadcasted_iota(jnp.int32, (rows, cells), 0)

    def along_x(field):
        return (pltpu.roll(field, cells - 1, 1) - pltpu.roll(field, 1, 1)) * 0.5

    def along_y(field, first, last):
        later = jnp.where(row == rows - 1, last, pltpu.roll(field, rows - 1, 0))
        earlier = jnp.where(row == 0, first, pltpu.roll(field, 1, 0))
        return (later - earlier) * 0.5

    east, north, turning = east_ref[...], north_ref[...], turning_ref[...]
    north_y = along_y(north, before_ref[:1], after_ref[:1])
    out_ref[0] = along_x(east) + north_y + upward_ref[...] - below_ref[...]
    out_ref[1] = turning * north - along_x(geopotential)
    out_ref[2] = turning * east + along_y(geopotential, rims[0], rims[1])


def on_device(forcing, spectral_weight, point_weight, point_bias, decoder, coriolis, layer_depth):
    level_count, channels, rows, cells = forcing.shape
    assert level_count == 1
    forcing = forcing[0]
    slices = lax.axis_size("gy")
    peers = slices // 2
    own = spectral_weight.shape[1]
    modes = own * slices
    ymodes = spectral_weight.shape[4]
    total_rows = rows * slices
    pack = LANES // (4 * own)
    groups = channels // pack
    part = groups // CHUNKS
    size = channels // CHUNKS
    wide = peers * 4 * own
    me = jnp.stack([lax.axis_index("gy"), lax.axis_index("lev")]).astype(jnp.int32)

    forward_x, inverse_x = x_tables(cells, modes, slices, cells * total_rows)
    smem = pl.BlockSpec(memory_space=pltpu.SMEM)
    vmem = pl.BlockSpec(memory_space=pltpu.VMEM)

    def whole(shape):
        return pl.BlockSpec(shape, lambda i: (0,) * len(shape))

    def params(mib, *grid):
        return pltpu.CompilerParams(dimension_semantics=grid, vmem_limit_bytes=mib << 20)


    block = next(b for b in (16, 8, rows) if rows % b == 0)
    blocks = 1
    many = next(b for b in (4, 2, 1) if part % b == 0)

    near_table = pl.pallas_call(
        functools.partial(forward_table_kernel, own, peers),
        grid=(1,),
        in_specs=[smem, whole((cells, wide))],
        out_specs=whole((cells, wide)),
        out_shape=jax.ShapeDtypeStruct((cells, wide), BF),
        compiler_params=params(6, "arbitrary"),
        cost_estimate=cost(2 * cells * wide * wide, 4 * cells * wide),
        name="forward_table",
    )(me, jnp.asarray(forward_x))
    spread_table, row_table = pl.pallas_call(
        functools.partial(other_tables_kernel, own, peers),
        grid=(1,),
        in_specs=[smem, whole((wide, cells)), whole((slices, rows, 2 * ymodes))],
        out_specs=[whole((wide, cells)), whole((peers * rows, 2 * ymodes))],
        out_shape=[
            jax.ShapeDtypeStruct((wide, cells), BF),
            jax.ShapeDtypeStruct((peers * rows, 2 * ymodes), BF),
        ],
        compiler_params=params(8, "arbitrary"),
        cost_estimate=cost(2 * cells * wide * wide, 4 * cells * wide),
        name="other_tables",
    )(me, jnp.asarray(inverse_x), jnp.asarray(y_table(total_rows, ymodes, slices)))
    square, bias, decoder_splat = pl.pallas_call(
        functools.partial(small_kernel, block),
        in_specs=[vmem] * 3,
        out_specs=[vmem] * 3,
        out_shape=[
            jax.ShapeDtypeStruct((channels * block, channels * block), BF),
            jax.ShapeDtypeStruct((channels * block, 1), F32),
            jax.ShapeDtypeStruct((channels * decoder.shape[0], LANES), F32),
        ],
        compiler_params=params(8),
        cost_estimate=cost(2 * channels * (channels * block) ** 2, 1 << 20),
        name="small",
    )(point_weight, point_bias[None, :], decoder)

    def swap(value, distance):
        return lax.ppermute(value, "gy", [(g, g ^ distance) for g in range(slices)])

    cells_spec = pl.BlockSpec((many * pack, rows, cells), lambda i: (i, 0, 0))
    lane_spec = pl.BlockSpec((many, rows, LANES), lambda i: (i, 0, 0))
    lane_shape = jax.ShapeDtypeStruct((part, rows, LANES), BF)
    mode_spec = pl.BlockSpec((many * pack, own, 2 * ymodes), lambda i: (i, 0, 0))
    tile = size * rows * cells

    def offset_spec(n):
        return pl.BlockSpec((many * pack, rows, cells), lambda i: (i + n * (part // many), 0, 0))

    def near_of(n):
        return pl.pallas_call(
            functools.partial(near_kernel, pack),
            grid=(part // many,),
            in_specs=[offset_spec(n), whole((cells, wide))],
            out_specs=[lane_spec] * peers,
            out_shape=[lane_shape] * peers,
            compiler_params=params(6, "arbitrary"),
            cost_estimate=cost(2 * tile * wide, tile * 2),
            name="near",
        )(pltpu.with_memory_space_constraint(forcing, pltpu.HBM), near_table)

    def exchange(parts):
        return [parts[0]] + [swap(parts[d], d) for d in range(1, peers)]

    def forward_y(parts):
        return pl.pallas_call(
            functools.partial(forward_y_kernel, pack, own, peers),
            grid=(part // many,),
            in_specs=[lane_spec] * peers + [whole(row_table.shape)],
            out_specs=[mode_spec] * 2,
            out_shape=[
                jax.ShapeDtypeStruct((size, own, 2 * ymodes), F32),
                jax.ShapeDtypeStruct((size, own, 2 * ymodes), BF),
            ],
            compiler_params=params(8, "arbitrary"),
            cost_estimate=cost(4 * part * LANES * peers * rows * ymodes, 2 * size * rows * wide),
            name="forward_y",
        )(*parts, row_table)

    def mix(kept, got, n, earlier):
        total = jax.ShapeDtypeStruct((own, channels, 2 * ymodes), F32)
        ends = [jax.ShapeDtypeStruct((size, own, 2 * ymodes), BF)] * CHUNKS
        final = n == CHUNKS - 1
        return pl.pallas_call(
            functools.partial(mix_kernel, n, CHUNKS),
            in_specs=[vmem] * (3 + len(earlier)),
            out_specs=[vmem] * len(ends) if final else [vmem],
            out_shape=ends if final else [total],
            scratch_shapes=[pltpu.VMEM((own, size, 2 * ymodes), F32)],
            compiler_params=params(8),
            cost_estimate=cost(
                8 * own * channels * size * ymodes, 4 * own * channels * size * ymodes
            ),
            name="mix",
        )(kept, got, spectral_weight, *earlier)

    def inverse_y(mine, theirs):
        return pl.pallas_call(
            functools.partial(inverse_y_kernel, pack, peers),
            grid=(part // many,),
            in_specs=[mode_spec] * 2 + [whole(row_table.shape)],
            out_specs=[lane_spec] * peers,
            out_shape=[lane_shape] * peers,
            compiler_params=params(8, "arbitrary"),
            cost_estimate=cost(4 * part * LANES * peers * rows * ymodes, 2 * size * rows * wide),
            name="inverse_y",
        )(mine, theirs, row_table)

    def pointwise(states):
        if len(states) == 1:
            specs = [pl.BlockSpec((channels, blocks * block, cells), lambda i: (0, i, 0))]
        else:
            specs = [pl.BlockSpec((size, blocks * block, cells), lambda i: (0, i, 0))] * CHUNKS
        return pl.pallas_call(
            functools.partial(pointwise_kernel, len(states), block),
            grid=(rows // (blocks * block),),
            in_specs=specs
            + [
                pl.BlockSpec((channels, blocks * block, cells), lambda i: (0, i, 0)),
                whole(square.shape),
                whole(bias.shape),
            ],
            out_specs=pl.BlockSpec((channels, blocks * block, cells), lambda i: (0, i, 0)),
            out_shape=jax.ShapeDtypeStruct((channels, rows, cells), F32),
            compiler_params=params(11, "arbitrary"),
            cost_estimate=cost(
                2 * channels * block * channels * rows * cells, 8 * channels * rows * cells
            ),
            name="pointwise",
        )(*states, forcing, square, bias)

    def update(backs, point, n):
        out = pl.pallas_call(
            functools.partial(update_kernel, pack, peers),
            grid=(part // many,),
            in_specs=[lane_spec] * peers
            + [offset_spec(n), whole(spread_table.shape), whole(near_table.shape)],
            out_specs=[cells_spec] + [lane_spec] * peers,
            out_shape=[jax.ShapeDtypeStruct((size, rows, cells), BF)] + [lane_shape] * peers,
            compiler_params=params(16, "arbitrary"),
            cost_estimate=cost(4 * tile * wide, 6 * tile, tile),
            name="update",
        )(*backs, point, spread_table, near_table)
        return out[0], out[1:]

    few = next(b for b in (2, 1) if part % b == 0)
    few_lanes = pl.BlockSpec((few, rows, LANES), lambda i: (i, 0, 0))

    def few_spec(n):
        return pl.BlockSpec(
            (few * pack, rows, cells), lambda i: (i + n * (part // few), 0, 0)
        )

    def last(backs, point, n, earlier):
        kinds = decoder.shape[0]
        more = [whole((rows, cells))] * kinds
        return pl.pallas_call(
            functools.partial(last_kernel, pack, peers, n * size, kinds),
            grid=(part // few,),
            in_specs=[few_lanes] * peers
            + [
                smem,
                smem,
                few_spec(n),
                whole(spread_table.shape),
                whole(decoder_splat.shape),
            ]
            + ([pl.BlockSpec(memory_space=pl.ANY)] + more if earlier else []),
            out_specs=[few_spec(n)] + more + [whole((2, cells))] * 2,
            out_shape=[jax.ShapeDtypeStruct((channels, rows, cells), F32)]
            + [jax.ShapeDtypeStruct((rows, cells), F32)] * kinds
            + [jax.ShapeDtypeStruct((2, cells), F32)] * 2,
            input_output_aliases={peers + 5: 0} if earlier else {},
            compiler_params=params(18, "arbitrary"),
            cost_estimate=cost(2 * tile * wide, 8 * tile, tile),
            name="last",
        )(*backs, me, layer_depth, point, spread_table, decoder_splat, *earlier[: kinds + 1])

    every = range(CHUNKS)
    nears = [near_of(n) for n in every]
    states = [forcing]
    for iteration in range(ITERS):
        arrived = [exchange(parts) for parts in nears]
        point = pointwise(states)
        halves = [forward_y(parts) for parts in arrived]
        kept = [half[0] for half in halves]
        got = [swap(half[1], peers) for half in halves]
        mixed = []
        for n in every:
            mixed = mix(kept[n], got[n], n, mixed)
        theirs = []
        for n in every:
            theirs.append(swap(mixed[n], peers))
        backs = [exchange(inverse_y(mixed[n], theirs[n])) for n in every]
        if iteration < ITERS - 1:
            done = [update(backs[n], point, n) for n in every]
            states = [pair[0] for pair in done]
            nears = [pair[1] for pair in done]
    done = []
    for n in every:
        done = last(backs[n], point, n, done)
    updated, east, north, upward, layer, low, high = done

    levels = lax.axis_size("lev")

    def from_below(value, step):
        return lax.ppermute(value, "lev", [(s, s + step) for s in range(levels - step)])

    up = [(i, (i + 1) % slices) for i in range(slices)]
    down = [(j, i) for i, j in up]
    pairs = levels % 2 == 0 and rows % 16 == 0
    if pairs:
        partner = [(s, s ^ 1) for s in range(levels)]
        other = lax.ppermute(layer, "lev", partner)
    below = from_below(upward, 1)
    before = lax.ppermute(high, "gy", up)
    after = lax.ppermute(low, "gy", down)
    if pairs:
        both = pl.pallas_call(
            pair_kernel,
            in_specs=[smem, vmem, vmem],
            out_specs=vmem,
            out_shape=jax.ShapeDtypeStruct((rows // 2, cells), F32),
            compiler_params=params(2),
            cost_estimate=cost(rows * cells, 8 * rows * cells),
            name="pair",
        )(me, layer, other)
        lower = from_below(both, 2)
        step = 2
        while step < levels - 2:
            lower = lower + from_below(lower, step)
            step *= 2
        lowers = [me, other, lower, lax.ppermute(lower, "lev", partner)]
    else:
        lowers = [from_below(layer, step) for step in range(1, levels)]
    rims = jnp.concatenate([before[1:], after[1:]], 0)
    shifts = [from_below(rims, step) for step in range(1, levels)]
    residual = pl.pallas_call(
        functools.partial(residual_kernel, pairs, len(shifts)),
        in_specs=[vmem] * (8 + len(shifts))
        + ([smem] if pairs else [vmem])
        + [vmem] * (len(lowers) - 1),
        out_specs=vmem,
        out_shape=jax.ShapeDtypeStruct((3, rows, cells), F32),
        compiler_params=params(10),
        cost_estimate=cost(20 * rows * cells, 36 * rows * cells),
        name="residual",
    )(east, north, upward, layer, below, before, after, *shifts, coriolis[:, None], *lowers)
    return updated[None], residual[:, None]


def solution(mesh):
    return jax.shard_map(
        on_device,
        mesh=mesh,
        in_specs=(
            P("lev", None, "gy", None),
            P(None, "gy", None, None, None),
            P(),
            P(),
            P(),
            P("gy"),
            P(),
        ),
        out_specs=(P("lev", None, "gy", None), P(None, "lev", "gy", None)),
        check_vma=False,
    )
```

```python
import functools
import math

import jax
import jax.numpy as jnp
import numpy as np
from jax import lax
from jax.experimental import pallas as pl
from jax.experimental.pallas import tpu as pltpu
from jax.sharding import PartitionSpec as P


ITERS = 3
CHUNKS = 2
BF = jnp.bfloat16
F32 = jnp.float32
LANES = 128


def cost(flops, bytes_accessed, transcendentals=0):
    return pl.CostEstimate(
        flops=int(flops), bytes_accessed=int(bytes_accessed), transcendentals=int(transcendentals)
    )


def turned(rows, cols, length):
    phase = (rows[:, None] * cols[None, :]) % length
    return phase.astype(np.float32) * np.float32(2.0 * math.pi / length)


def x_tables(cells, modes, slices, total):
    angle = turned(np.arange(modes, dtype=np.int64), np.arange(cells, dtype=np.int64), cells)
    pair = np.stack([np.cos(angle), -np.sin(angle)], 0).astype(np.float32)
    factor = (np.where(np.arange(modes) == 0, 1.0, 2.0).astype(np.float32) / np.float32(total))
    inverse = pair * factor[None, :, None]
    own = modes // slices

    def by_slice(table):
        table = table.reshape(2, slices, own, cells).transpose(1, 0, 2, 3)
        return table.reshape(slices, 2 * own, cells).astype(BF)

    order = [d + h * (slices // 2) for d in range(slices // 2) for h in range(2)]
    first, second = [by_slice(table)[order].reshape(-1, cells) for table in (pair, inverse)]
    return np.ascontiguousarray(first.T), second


def y_table(rows, modes, slices):
    index = np.arange(modes, dtype=np.int64)
    signed = np.where(index < modes // 2, index, index + (rows - modes))
    angle = turned(np.arange(rows, dtype=np.int64), signed, rows)
    both = np.concatenate([np.cos(angle), np.sin(angle)], 1).astype(np.float32)
    return both.reshape(slices, rows // slices, 2 * modes).astype(BF)


def dot(a, b, dims):
    return lax.dot_general(a, b, (dims, ((), ())), preferred_element_type=F32)


def store_near(state, table, near_refs, pack, rows, first=0):
    width = LANES // pack
    near = dot(state, table, ((1,), (0,)))
    for g in range(state.shape[0] // (pack * rows)):
        for d, ref in enumerate(near_refs):
            parts = []
            for j in range(pack):
                at = (g * pack + j) * rows
                parts.append(near[at : at + rows, d * width : (d + 1) * width])
            ref[first + g] = jnp.concatenate(parts, 1).astype(BF)


def near_kernel(pack, state_ref, table_ref, *near_refs):
    count, rows, cells = state_ref.shape
    state = state_ref[...].reshape(count * rows, cells)
    store_near(state, table_ref[...], near_refs, pack, rows)


def slice_order(own, peers, me, across, along):
    wide = peers * 4 * own
    block = 2 * own
    mask = ((me % peers) * 2) | (me // peers)
    place = lax.broadcasted_iota(jnp.int32, (wide, wide), across)
    source = ((place // block) ^ mask) * block + place % block
    return (lax.broadcasted_iota(jnp.int32, (wide, wide), along) == source).astype(BF)


def forward_table_kernel(own, peers, me_ref, forward_ref, near_ref):
    order = slice_order(own, peers, me_ref[0], 1, 0)
    near_ref[...] = dot(forward_ref[...], order, ((1,), (0,))).astype(BF)


def other_tables_kernel(own, peers, me_ref, inverse_ref, row_ref, spread_ref, rows_ref):
    order = slice_order(own, peers, me_ref[0], 0, 1)
    spread_ref[...] = dot(order, inverse_ref[...], ((1,), (0,))).astype(BF)
    rows = row_ref.shape[1]
    for d in range(peers):
        rows_ref[d * rows : (d + 1) * rows] = row_ref[me_ref[0] ^ d]


def small_kernel(block, weight_ref, bias_ref, decoder_ref, square_ref, column_ref, splat_ref):
    channels = weight_ref.shape[0]
    count = channels * block
    row = lax.broadcasted_iota(jnp.int32, (count, channels), 0) // block
    mine = row == lax.broadcasted_iota(jnp.int32, (count, channels), 1)
    pick = mine.astype(BF)
    left = dot(pick, weight_ref[...], ((1,), (1,))).astype(BF)
    full = dot(left, pick, ((1,), (1,)))
    down = lax.broadcasted_iota(jnp.int32, (count, count), 0) % block
    across = lax.broadcasted_iota(jnp.int32, (count, count), 1) % block
    square_ref[...] = jnp.where(down == across, full, 0.0).astype(BF)
    column_ref[...] = jnp.sum(jnp.where(mine, bias_ref[...], 0.0), 1, keepdims=True)
    fields = decoder_ref.shape[0]
    lines = channels * fields
    row = lax.broadcasted_iota(jnp.int32, (lines, channels), 0) // fields
    pick = (row == lax.broadcasted_iota(jnp.int32, (lines, channels), 1)).astype(BF)
    values = dot(pick, decoder_ref[...], ((1,), (1,)))
    row = lax.broadcasted_iota(jnp.int32, (lines, fields), 0) % fields
    own = row == lax.broadcasted_iota(jnp.int32, (lines, fields), 1)
    value = jnp.sum(jnp.where(own, values, 0.0), 1, keepdims=True)
    splat_ref[...] = jnp.broadcast_to(value, splat_ref.shape)


def forward_y_kernel(pack, own, peers, *refs):
    near_refs, (table_ref, keep_ref, send_ref) = refs[:peers], refs[peers:]
    modes = table_ref.shape[1] // 2
    for g in range(near_refs[0].shape[0]):
        near = jnp.concatenate([ref[g] for ref in near_refs], 0)
        both = dot(near, table_ref[...], ((0,), (0,)))
        for j in range(pack):
            for h, out_ref in ((0, keep_ref), (1, send_ref)):
                at = (j * 2 + h) * 2 * own
                real = both[at : at + own]
                imag = both[at + own : at + 2 * own]
                c = g * pack + j
                out_ref[c, :, :modes] = (real[:, :modes] + imag[:, modes:]).astype(out_ref.dtype)
                out_ref[c, :, modes:] = (imag[:, :modes] - real[:, modes:]).astype(out_ref.dtype)


def mix_kernel(n, chunks, *refs):
    keep_ref, got_ref, weight_ref = refs[:3]
    earlier = refs[3:4] if n > 0 else ()
    out_refs = refs[3 + len(earlier) : -1]
    spectrum = refs[-1]
    own, channels, modes = weight_ref.shape[1], weight_ref.shape[2], weight_ref.shape[4]
    size = channels // chunks
    value = keep_ref[...] + got_ref[...].astype(F32)
    spectrum[...] = jnp.swapaxes(value, 0, 1)
    total = out_refs[0] if n < chunks - 1 else earlier[0]

    def step(k, carry):
        row = spectrum[k]
        zero = jnp.zeros((channels, modes), F32)
        real, imag = [zero, zero], [zero, zero]
        if earlier:
            real[0], imag[0] = earlier[0][k, :, :modes], earlier[0][k, :, modes:]
        for i in range(size):
            s0, s1 = row[i : i + 1, :modes], row[i : i + 1, modes:]
            w0 = weight_ref[0, k, n * size + i].astype(F32)
            w1 = weight_ref[1, k, n * size + i].astype(F32)
            real[i % 2] = real[i % 2] + (s0 * w0 - s1 * w1)
            imag[i % 2] = imag[i % 2] + (s0 * w1 + s1 * w0)
        total[k, :, :modes] = real[0] + real[1]
        total[k, :, modes:] = imag[0] + imag[1]
        return carry

    lax.fori_loop(0, own, step, 0)
    if n == chunks - 1:
        for c in range(chunks):
            part = jnp.swapaxes(total[:, c * size : (c + 1) * size], 0, 1)
            out_refs[c][...] = part.astype(BF)


def inverse_y_kernel(pack, peers, mine_ref, theirs_ref, table_ref, *back_refs):
    rows, modes = table_ref.shape[0] // peers, table_ref.shape[1] // 2
    for g in range(back_refs[0].shape[0]):
        parts = []
        for j in range(pack):
            for ref in (mine_ref, theirs_ref):
                value = ref[g * pack + j].astype(F32)
                real, imag = value[:, :modes], value[:, modes:]
                parts.append(jnp.concatenate([real, -imag], 1))
                parts.append(jnp.concatenate([imag, real], 1))
        turned_modes = jnp.concatenate(parts, 0).astype(BF)
        back = dot(table_ref[...], turned_modes, ((1,), (1,)))
        for d in range(peers):
            back_refs[d][g] = back[d * rows : (d + 1) * rows].astype(BF)


def gelu(x):
    scale = math.sqrt(2.0 / math.pi)
    half = 0.5 * x
    return half + half * jnp.tanh(x * (scale + (scale * 0.044715) * (x * x)))


def spread_of(pack, back_refs, table_ref):
    width = LANES // pack
    blocks = []
    for g in range(back_refs[0].shape[0]):
        values = [ref[g].astype(F32) for ref in back_refs]
        for j in range(pack):
            lanes = [v[:, j * width : (j + 1) * width] for v in values]
            blocks.append(jnp.concatenate(lanes, 1).astype(BF))
    return dot(jnp.concatenate(blocks, 0), table_ref[...], ((1,), (0,)))


def update_kernel(pack, peers, *refs):
    back_refs, (point_ref, inverse_ref, forward_ref) = refs[:peers], refs[peers : peers + 3]
    state_ref, near_refs = refs[peers + 3], refs[peers + 4 :]
    count, rows, cells = state_ref.shape
    point = point_ref[...].reshape(count * rows, cells)
    updated = gelu(spread_of(pack, back_refs, inverse_ref) + point)
    state = updated.astype(BF)
    state_ref[...] = state.reshape(count, rows, cells)
    store_near(state, forward_ref[...], near_refs, pack, rows)


def last_kernel(pack, peers, first, kinds, *refs):
    back_refs = refs[:peers]
    me_ref, depth_ref, point_ref, inverse_ref, decoder_ref = refs[peers : peers + 5]
    updated_ref, *field_refs = refs[-kinds - 3 : -2]
    earlier = refs[peers + 5 : -kinds - 3]
    low_ref, high_ref = refs[-2:]
    count, rows, cells = updated_ref.shape
    group = pl.program_id(0)
    point = point_ref[...].reshape(count * rows, cells)
    updated = gelu(spread_of(pack, back_refs, inverse_ref) + point)
    updated_ref[...] = updated.reshape(count, rows, cells)

    @pl.when(group == 0)
    def _():
        for f in range(kinds):
            field_refs[f][...] = (
                earlier[1 + f][...] if earlier else jnp.zeros((rows, cells), F32)
            )

    lanes = next(b for b in (LANES, cells) if cells % b == 0)
    depth = depth_ref[me_ref[1]]
    weights = []
    for f in range(kinds):
        lines = [
            decoder_ref[pl.ds((first + group * count + c) * kinds + f, 1), :]
            for c in range(count)
        ]
        lines = [line * depth for line in lines] if f == kinds - 1 else lines
        weights.append([jnp.broadcast_to(line, (8, lanes)) for line in lines])

    def slab(t, carry):
        at = pl.ds(pl.multiple_of(t * 8, 8), 8)
        for start in range(0, cells, lanes):
            to = slice(start, start + lanes)
            values = [updated_ref[c, at, to] for c in range(count)]
            for f in range(kinds):
                terms = [weights[f][c] * values[c] for c in range(count)]
                while len(terms) > 1:
                    terms = [sum(terms[i + 1 : i + 2], terms[i]) for i in range(0, len(terms), 2)]
                field_refs[f][at, to] += terms[0]
        return carry

    lax.fori_loop(0, rows // 8, slab, 0)

    @pl.when(group == pl.num_programs(0) - 1)
    def _():
        for i, f in enumerate((1, kinds - 1)):
            low_ref[i : i + 1] = field_refs[f][:1]
            high_ref[i : i + 1] = field_refs[f][rows - 1 :]


def pair_kernel(me_ref, layer_ref, other_ref, rims_ref, other_rims_ref, both_ref):
    half = layer_ref.shape[0] // 2
    at = pl.ds(pl.multiple_of((me_ref[1] & 1) * half, 8), half)
    both_ref[:half] = layer_ref[at, :] + other_ref[at, :]
    both_ref[half : half + 2] = rims_ref[...] + other_rims_ref[...]
    both_ref[half + 2 :] = jnp.zeros((both_ref.shape[0] - half - 2, both_ref.shape[1]), F32)


def pointwise_kernel(chunks, block, *refs):
    state_refs, (forcing_ref, weight_ref, bias_ref, out_ref) = refs[:chunks], refs[chunks:]
    channels, rows, cells = out_ref.shape
    count = channels * block
    for t in range(rows // block):
        at = slice(t * block, (t + 1) * block)
        state = jnp.concatenate([ref[:, at] for ref in state_refs], 0).reshape(count, cells)
        source = forcing_ref[:, at].reshape(count, cells).astype(F32) + bias_ref[...]
        out = dot(weight_ref[...], state, ((1,), (0,))) + source
        out_ref[:, at] = out.reshape(channels, block, cells)


def residual_kernel(paired, *refs):
    east_ref, north_ref, upward_ref, layer_ref, below_ref, before_ref, after_ref = refs[:7]
    turning_ref, rims_ref, rest, out_ref = refs[7], refs[8], refs[9:-1], refs[-1]
    rows, cells = layer_ref.shape
    geopotential = layer_ref[...]
    rims = rims_ref[...]
    if paired:
        me_ref, other_ref, other_rims_ref, mine_ref, partner_ref = rest
        odd = (me_ref[1] & 1) == 1
        half = rows // 2
        mine, theirs = mine_ref[:half], partner_ref[:half]
        lower = jnp.concatenate(
            [jnp.where(odd, theirs, mine), jnp.where(odd, mine, theirs)], 0
        )
        geopotential = geopotential + jnp.where(odd, other_ref[...], 0.0) + lower
        rims = rims + jnp.where(odd, other_rims_ref[...], 0.0) + mine_ref[half : half + 2]
    else:
        count = len(rest) // 2
        for ref in rest[:count]:
            geopotential = geopotential + ref[...]
        for ref in rest[count:]:
            rims = rims + ref[...]
    rims = [rims[:1], rims[1:]]
    row = lax.broadcasted_iota(jnp.int32, (rows, cells), 0)

    def along_x(field):
        return (pltpu.roll(field, cells - 1, 1) - pltpu.roll(field, 1, 1)) * 0.5

    def along_y(field, first, last):
        later = jnp.where(row == rows - 1, last, pltpu.roll(field, rows - 1, 0))
        earlier = jnp.where(row == 0, first, pltpu.roll(field, 1, 0))
        return (later - earlier) * 0.5

    east, north, turning = east_ref[...], north_ref[...], turning_ref[...]
    north_y = along_y(north, before_ref[:1], after_ref[:1])
    out_ref[0] = along_x(east) + north_y + upward_ref[...] - below_ref[...]
    out_ref[1] = turning * north - along_x(geopotential)
    out_ref[2] = turning * east + along_y(geopotential, rims[0], rims[1])


def on_device(forcing, spectral_weight, point_weight, point_bias, decoder, coriolis, layer_depth):
    level_count, channels, rows, cells = forcing.shape
    assert level_count == 1
    forcing = forcing[0]
    slices = lax.axis_size("gy")
    peers = slices // 2
    own = spectral_weight.shape[1]
    modes = own * slices
    ymodes = spectral_weight.shape[4]
    total_rows = rows * slices
    pack = LANES // (4 * own)
    groups = channels // pack
    part = groups // CHUNKS
    size = channels // CHUNKS
    wide = peers * 4 * own
    me = jnp.stack([lax.axis_index("gy"), lax.axis_index("lev")]).astype(jnp.int32)

    forward_x, inverse_x = x_tables(cells, modes, slices, cells * total_rows)
    smem = pl.BlockSpec(memory_space=pltpu.SMEM)
    vmem = pl.BlockSpec(memory_space=pltpu.VMEM)

    def whole(shape):
        return pl.BlockSpec(shape, lambda i: (0,) * len(shape))

    def params(mib, *grid):
        return pltpu.CompilerParams(dimension_semantics=grid, vmem_limit_bytes=mib << 20)


    block = next(b for b in (16, 8, rows) if rows % b == 0)
    blocks = 1
    many = next(b for b in (4, 2, 1) if part % b == 0)

    near_table = pl.pallas_call(
        functools.partial(forward_table_kernel, own, peers),
        grid=(1,),
        in_specs=[smem, whole((cells, wide))],
        out_specs=whole((cells, wide)),
        out_shape=jax.ShapeDtypeStruct((cells, wide), BF),
        compiler_params=params(6, "arbitrary"),
        cost_estimate=cost(2 * cells * wide * wide, 4 * cells * wide),
        name="forward_table",
    )(me, jnp.asarray(forward_x))
    spread_table, row_table = pl.pallas_call(
        functools.partial(other_tables_kernel, own, peers),
        grid=(1,),
        in_specs=[smem, whole((wide, cells)), whole((slices, rows, 2 * ymodes))],
        out_specs=[whole((wide, cells)), whole((peers * rows, 2 * ymodes))],
        out_shape=[
            jax.ShapeDtypeStruct((wide, cells), BF),
            jax.ShapeDtypeStruct((peers * rows, 2 * ymodes), BF),
        ],
        compiler_params=params(8, "arbitrary"),
        cost_estimate=cost(2 * cells * wide * wide, 4 * cells * wide),
        name="other_tables",
    )(me, jnp.asarray(inverse_x), jnp.asarray(y_table(total_rows, ymodes, slices)))
    square, bias, decoder_splat = pl.pallas_call(
        functools.partial(small_kernel, block),
        in_specs=[vmem] * 3,
        out_specs=[vmem] * 3,
        out_shape=[
            jax.ShapeDtypeStruct((channels * block, channels * block), BF),
            jax.ShapeDtypeStruct((channels * block, 1), F32),
            jax.ShapeDtypeStruct((channels * decoder.shape[0], LANES), F32),
        ],
        compiler_params=params(8),
        cost_estimate=cost(2 * channels * (channels * block) ** 2, 1 << 20),
        name="small",
    )(point_weight, point_bias[None, :], decoder)

    def swap(value, distance):
        return lax.ppermute(value, "gy", [(g, g ^ distance) for g in range(slices)])

    cells_spec = pl.BlockSpec((many * pack, rows, cells), lambda i: (i, 0, 0))
    lane_spec = pl.BlockSpec((many, rows, LANES), lambda i: (i, 0, 0))
    lane_shape = jax.ShapeDtypeStruct((part, rows, LANES), BF)
    mode_spec = whole((size, own, 2 * ymodes))
    part_spec = whole((part, rows, LANES))
    tile = size * rows * cells

    def offset_spec(n):
        return pl.BlockSpec((many * pack, rows, cells), lambda i: (i + n * (part // many), 0, 0))

    def near_of(n):
        return pl.pallas_call(
            functools.partial(near_kernel, pack),
            grid=(part // many,),
            in_specs=[offset_spec(n), whole((cells, wide))],
            out_specs=[lane_spec] * peers,
            out_shape=[lane_shape] * peers,
            compiler_params=params(6, "arbitrary"),
            cost_estimate=cost(2 * tile * wide, tile * 2),
            name="near",
        )(pltpu.with_memory_space_constraint(forcing, pltpu.HBM), near_table)

    def exchange(parts):
        return [parts[0]] + [swap(parts[d], d) for d in range(1, peers)]

    def forward_y(parts):
        return pl.pallas_call(
            functools.partial(forward_y_kernel, pack, own, peers),
            grid=(1,),
            in_specs=[part_spec] * peers + [whole(row_table.shape)],
            out_specs=[mode_spec] * 2,
            out_shape=[
                jax.ShapeDtypeStruct((size, own, 2 * ymodes), F32),
                jax.ShapeDtypeStruct((size, own, 2 * ymodes), BF),
            ],
            compiler_params=params(8, "arbitrary"),
            cost_estimate=cost(4 * part * LANES * peers * rows * ymodes, 2 * size * rows * wide),
            name="forward_y",
        )(*parts, row_table)

    def mix(kept, got, n, earlier):
        total = jax.ShapeDtypeStruct((own, channels, 2 * ymodes), F32)
        ends = [jax.ShapeDtypeStruct((size, own, 2 * ymodes), BF)] * CHUNKS
        final = n == CHUNKS - 1
        return pl.pallas_call(
            functools.partial(mix_kernel, n, CHUNKS),
            in_specs=[vmem] * (3 + len(earlier)),
            out_specs=[vmem] * len(ends) if final else [vmem],
            out_shape=ends if final else [total],
            scratch_shapes=[pltpu.VMEM((own, size, 2 * ymodes), F32)],
            compiler_params=params(8),
            cost_estimate=cost(
                8 * own * channels * size * ymodes, 4 * own * channels * size * ymodes
            ),
            name="mix",
        )(kept, got, spectral_weight, *earlier)

    def inverse_y(mine, theirs):
        return pl.pallas_call(
            functools.partial(inverse_y_kernel, pack, peers),
            grid=(1,),
            in_specs=[mode_spec] * 2 + [whole(row_table.shape)],
            out_specs=[part_spec] * peers,
            out_shape=[lane_shape] * peers,
            compiler_params=params(8, "arbitrary"),
            cost_estimate=cost(4 * part * LANES * peers * rows * ymodes, 2 * size * rows * wide),
            name="inverse_y",
        )(mine, theirs, row_table)

    def pointwise(states):
        if len(states) == 1:
            specs = [pl.BlockSpec((channels, blocks * block, cells), lambda i: (0, i, 0))]
        else:
            specs = [pl.BlockSpec((size, blocks * block, cells), lambda i: (0, i, 0))] * CHUNKS
        return pl.pallas_call(
            functools.partial(pointwise_kernel, len(states), block),
            grid=(rows // (blocks * block),),
            in_specs=specs
            + [
                pl.BlockSpec((channels, blocks * block, cells), lambda i: (0, i, 0)),
                whole(square.shape),
                whole(bias.shape),
            ],
            out_specs=pl.BlockSpec((channels, blocks * block, cells), lambda i: (0, i, 0)),
            out_shape=jax.ShapeDtypeStruct((channels, rows, cells), F32),
            compiler_params=params(11, "arbitrary"),
            cost_estimate=cost(
                2 * channels * block * channels * rows * cells, 8 * channels * rows * cells
            ),
            name="pointwise",
        )(*states, forcing, square, bias)

    def update(backs, point, n):
        out = pl.pallas_call(
            functools.partial(update_kernel, pack, peers),
            grid=(part // many,),
            in_specs=[lane_spec] * peers
            + [offset_spec(n), whole(spread_table.shape), whole(near_table.shape)],
            out_specs=[cells_spec] + [lane_spec] * peers,
            out_shape=[jax.ShapeDtypeStruct((size, rows, cells), BF)] + [lane_shape] * peers,
            compiler_params=params(16, "arbitrary"),
            cost_estimate=cost(4 * tile * wide, 6 * tile, tile),
            name="update",
        )(*backs, point, spread_table, near_table)
        return out[0], out[1:]

    few = next(b for b in (2, 1) if part % b == 0)
    few_lanes = pl.BlockSpec((few, rows, LANES), lambda i: (i, 0, 0))

    def few_spec(n):
        return pl.BlockSpec(
            (few * pack, rows, cells), lambda i: (i + n * (part // few), 0, 0)
        )

    def last(backs, point, n, earlier):
        kinds = decoder.shape[0]
        more = [whole((rows, cells))] * kinds
        return pl.pallas_call(
            functools.partial(last_kernel, pack, peers, n * size, kinds),
            grid=(part // few,),
            in_specs=[few_lanes] * peers
            + [
                smem,
                smem,
                few_spec(n),
                whole(spread_table.shape),
                whole(decoder_splat.shape),
            ]
            + ([pl.BlockSpec(memory_space=pl.ANY)] + more if earlier else []),
            out_specs=[few_spec(n)] + more + [whole((2, cells))] * 2,
            out_shape=[jax.ShapeDtypeStruct((channels, rows, cells), F32)]
            + [jax.ShapeDtypeStruct((rows, cells), F32)] * kinds
            + [jax.ShapeDtypeStruct((2, cells), F32)] * 2,
            input_output_aliases={peers + 5: 0} if earlier else {},
            compiler_params=params(18, "arbitrary"),
            cost_estimate=cost(2 * tile * wide, 8 * tile, tile),
            name="last",
        )(*backs, me, layer_depth, point, spread_table, decoder_splat, *earlier[: kinds + 1])

    every = range(CHUNKS)
    nears = [near_of(n) for n in every]
    states = [forcing]
    for iteration in range(ITERS):
        arrived = [exchange(parts) for parts in nears]
        point = pointwise(states)
        halves = [forward_y(parts) for parts in arrived]
        kept = [half[0] for half in halves]
        got = [swap(half[1], peers) for half in halves]
        mixed = []
        for n in every:
            mixed = mix(kept[n], got[n], n, mixed)
        theirs = []
        for n in every:
            theirs.append(swap(mixed[n], peers))
        backs = [exchange(inverse_y(mixed[n], theirs[n])) for n in every]
        if iteration < ITERS - 1:
            done = [update(backs[n], point, n) for n in every]
            states = [pair[0] for pair in done]
            nears = [pair[1] for pair in done]
    done = []
    for n in every:
        done = last(backs[n], point, n, done)
    updated, east, north, upward, layer, low, high = done

    levels = lax.axis_size("lev")

    def from_below(value, step):
        return lax.ppermute(value, "lev", [(s, s + step) for s in range(levels - step)])

    up = [(i, (i + 1) % slices) for i in range(slices)]
    down = [(j, i) for i, j in up]
    pairs = levels % 2 == 0 and rows % 16 == 0
    if pairs:
        partner = [(s, s ^ 1) for s in range(levels)]
        other = lax.ppermute(layer, "lev", partner)
    below = from_below(upward, 1)
    before = lax.ppermute(high, "gy", up)
    after = lax.ppermute(low, "gy", down)
    rims = jnp.concatenate([before[1:], after[1:]], 0)
    if pairs:
        other_rims = lax.ppermute(rims, "lev", partner)
        both = pl.pallas_call(
            pair_kernel,
            in_specs=[smem] + [vmem] * 4,
            out_specs=vmem,
            out_shape=jax.ShapeDtypeStruct((rows // 2 + 8, cells), F32),
            compiler_params=params(2),
            cost_estimate=cost(rows * cells, 8 * rows * cells),
            name="pair",
        )(me, layer, other, rims, other_rims)
        lower = from_below(both, 2)
        step = 2
        while step < levels - 2:
            lower = lower + from_below(lower, step)
            step *= 2
        lowers = [me, other, other_rims, lower, lax.ppermute(lower, "lev", partner)]
    else:
        lowers = [from_below(v, step) for v in (layer, rims) for step in range(1, levels)]
    residual = pl.pallas_call(
        functools.partial(residual_kernel, pairs),
        in_specs=[vmem] * 9
        + ([smem] if pairs else [vmem])
        + [vmem] * (len(lowers) - 1),
        out_specs=vmem,
        out_shape=jax.ShapeDtypeStruct((3, rows, cells), F32),
        compiler_params=params(10),
        cost_estimate=cost(20 * rows * cells, 36 * rows * cells),
        name="residual",
    )(
        east,
        north,
        upward,
        layer,
        below,
        before,
        after,
        coriolis[:, None],
        rims,
        *lowers,
    )
    return updated[None], residual[:, None]


def solution(mesh):
    return jax.shard_map(
        on_device,
        mesh=mesh,
        in_specs=(
            P("lev", None, "gy", None),
            P(None, "gy", None, None, None),
            P(),
            P(),
            P(),
            P("gy"),
            P(),
        ),
        out_specs=(P("lev", None, "gy", None), P(None, "lev", "gy", None)),
        check_vma=False,
    )
```

```python
import functools
import math

import jax
import jax.numpy as jnp
import numpy as np
from jax import lax
from jax.experimental import pallas as pl
from jax.experimental.pallas import tpu as pltpu
from jax.sharding import PartitionSpec as P


ITERS = 3
CHUNKS = 2
BF = jnp.bfloat16
F32 = jnp.float32
LANES = 128


def cost(flops, bytes_accessed, transcendentals=0):
    return pl.CostEstimate(
        flops=int(flops), bytes_accessed=int(bytes_accessed), transcendentals=int(transcendentals)
    )


def turned(rows, cols, length):
    phase = (rows[:, None] * cols[None, :]) % length
    return phase.astype(np.float32) * np.float32(2.0 * math.pi / length)


def x_tables(cells, modes, slices, total):
    angle = turned(np.arange(modes, dtype=np.int64), np.arange(cells, dtype=np.int64), cells)
    pair = np.stack([np.cos(angle), -np.sin(angle)], 0).astype(np.float32)
    factor = (np.where(np.arange(modes) == 0, 1.0, 2.0).astype(np.float32) / np.float32(total))
    inverse = pair * factor[None, :, None]
    own = modes // slices

    def by_slice(table):
        table = table.reshape(2, slices, own, cells).transpose(1, 0, 2, 3)
        return table.reshape(slices, 2 * own, cells).astype(BF)

    order = [d + h * (slices // 2) for d in range(slices // 2) for h in range(2)]
    first, second = [by_slice(table)[order].reshape(-1, cells) for table in (pair, inverse)]
    return np.ascontiguousarray(first.T), second


def y_table(rows, modes, slices):
    index = np.arange(modes, dtype=np.int64)
    signed = np.where(index < modes // 2, index, index + (rows - modes))
    angle = turned(np.arange(rows, dtype=np.int64), signed, rows)
    both = np.concatenate([np.cos(angle), np.sin(angle)], 1).astype(np.float32)
    return both.reshape(slices, rows // slices, 2 * modes).astype(BF)


def dot(a, b, dims):
    return lax.dot_general(a, b, (dims, ((), ())), preferred_element_type=F32)


def store_near(state, table, near_refs, pack, rows, first=0):
    width = LANES // pack
    near = dot(state, table, ((1,), (0,)))
    for g in range(state.shape[0] // (pack * rows)):
        for d, ref in enumerate(near_refs):
            parts = []
            for j in range(pack):
                at = (g * pack + j) * rows
                parts.append(near[at : at + rows, d * width : (d + 1) * width])
            ref[first + g] = jnp.concatenate(parts, 1).astype(BF)


def near_kernel(pack, state_ref, table_ref, *near_refs):
    count, rows, cells = state_ref.shape
    state = state_ref[...].reshape(count * rows, cells)
    store_near(state, table_ref[...], near_refs, pack, rows)


def slice_order(own, peers, me, across, along):
    wide = peers * 4 * own
    block = 2 * own
    mask = ((me % peers) * 2) | (me // peers)
    place = lax.broadcasted_iota(jnp.int32, (wide, wide), across)
    source = ((place // block) ^ mask) * block + place % block
    return (lax.broadcasted_iota(jnp.int32, (wide, wide), along) == source).astype(BF)


def forward_table_kernel(own, peers, me_ref, forward_ref, near_ref):
    order = slice_order(own, peers, me_ref[0], 1, 0)
    near_ref[...] = dot(forward_ref[...], order, ((1,), (0,))).astype(BF)


def other_tables_kernel(own, peers, me_ref, inverse_ref, row_ref, spread_ref, rows_ref):
    order = slice_order(own, peers, me_ref[0], 0, 1)
    spread_ref[...] = dot(order, inverse_ref[...], ((1,), (0,))).astype(BF)
    rows = row_ref.shape[1]
    for d in range(peers):
        rows_ref[d * rows : (d + 1) * rows] = row_ref[me_ref[0] ^ d]


def small_kernel(block, weight_ref, bias_ref, decoder_ref, square_ref, column_ref, splat_ref):
    channels = weight_ref.shape[0]
    count = channels * block
    row = lax.broadcasted_iota(jnp.int32, (count, channels), 0) // block
    mine = row == lax.broadcasted_iota(jnp.int32, (count, channels), 1)
    pick = mine.astype(BF)
    left = dot(pick, weight_ref[...], ((1,), (1,))).astype(BF)
    full = dot(left, pick, ((1,), (1,)))
    down = lax.broadcasted_iota(jnp.int32, (count, count), 0) % block
    across = lax.broadcasted_iota(jnp.int32, (count, count), 1) % block
    square_ref[...] = jnp.where(down == across, full, 0.0).astype(BF)
    column_ref[...] = jnp.sum(jnp.where(mine, bias_ref[...], 0.0), 1, keepdims=True)
    fields = decoder_ref.shape[0]
    lines = channels * fields
    row = lax.broadcasted_iota(jnp.int32, (lines, channels), 0) // fields
    pick = (row == lax.broadcasted_iota(jnp.int32, (lines, channels), 1)).astype(BF)
    values = dot(pick, decoder_ref[...], ((1,), (1,)))
    row = lax.broadcasted_iota(jnp.int32, (lines, fields), 0) % fields
    own = row == lax.broadcasted_iota(jnp.int32, (lines, fields), 1)
    value = jnp.sum(jnp.where(own, values, 0.0), 1, keepdims=True)
    splat_ref[...] = jnp.broadcast_to(value, splat_ref.shape)


def forward_y_kernel(pack, own, peers, *refs):
    near_refs, (table_ref, keep_ref, send_ref) = refs[:peers], refs[peers:]
    modes = table_ref.shape[1] // 2
    for g in range(near_refs[0].shape[0]):
        near = jnp.concatenate([ref[g] for ref in near_refs], 0)
        both = dot(near, table_ref[...], ((0,), (0,)))
        for j in range(pack):
            for h, out_ref in ((0, keep_ref), (1, send_ref)):
                at = (j * 2 + h) * 2 * own
                real = both[at : at + own]
                imag = both[at + own : at + 2 * own]
                c = g * pack + j
                out_ref[c, :, :modes] = (real[:, :modes] + imag[:, modes:]).astype(out_ref.dtype)
                out_ref[c, :, modes:] = (imag[:, :modes] - real[:, modes:]).astype(out_ref.dtype)


def mix_kernel(n, chunks, outputs, *refs):
    keep_ref, got_ref, weight_ref = refs[:3]
    earlier_ref = refs[3] if n > 0 else None
    out_ref, spectrum, mixed = refs[-3:]
    own, channels, modes = weight_ref.shape[1], weight_ref.shape[2], weight_ref.shape[4]
    size = channels // chunks
    value = keep_ref[...] + got_ref[...].astype(F32)
    spectrum[...] = jnp.swapaxes(value, 0, 1)
    final = n == chunks - 1
    total = mixed if final else out_ref

    def step(k, carry):
        row = spectrum[k]
        zero = jnp.zeros((outputs.stop - outputs.start, modes), F32)
        real, imag = [zero, zero], [zero, zero]
        if n > 0:
            real[0] = earlier_ref[k, outputs, :modes]
            imag[0] = earlier_ref[k, outputs, modes:]
        for i in range(size):
            s0, s1 = row[i : i + 1, :modes], row[i : i + 1, modes:]
            w0 = weight_ref[0, k, n * size + i, outputs].astype(F32)
            w1 = weight_ref[1, k, n * size + i, outputs].astype(F32)
            real[i % 2] = real[i % 2] + (s0 * w0 - s1 * w1)
            imag[i % 2] = imag[i % 2] + (s0 * w1 + s1 * w0)
        total[k, :, :modes] = real[0] + real[1]
        total[k, :, modes:] = imag[0] + imag[1]
        return carry

    lax.fori_loop(0, own, step, 0)
    if final:
        out_ref[...] = jnp.swapaxes(mixed[...], 0, 1).astype(BF)


def inverse_y_kernel(pack, peers, mine_ref, theirs_ref, table_ref, *back_refs):
    rows, modes = table_ref.shape[0] // peers, table_ref.shape[1] // 2
    for g in range(back_refs[0].shape[0]):
        parts = []
        for j in range(pack):
            for ref in (mine_ref, theirs_ref):
                value = ref[g * pack + j].astype(F32)
                real, imag = value[:, :modes], value[:, modes:]
                parts.append(jnp.concatenate([real, -imag], 1))
                parts.append(jnp.concatenate([imag, real], 1))
        turned_modes = jnp.concatenate(parts, 0).astype(BF)
        back = dot(table_ref[...], turned_modes, ((1,), (1,)))
        for d in range(peers):
            back_refs[d][g] = back[d * rows : (d + 1) * rows].astype(BF)


def gelu(x):
    scale = math.sqrt(2.0 / math.pi)
    half = 0.5 * x
    return half + half * jnp.tanh(x * (scale + (scale * 0.044715) * (x * x)))


def spread_of(pack, back_refs, table_ref):
    width = LANES // pack
    blocks = []
    for g in range(back_refs[0].shape[0]):
        values = [ref[g].astype(F32) for ref in back_refs]
        for j in range(pack):
            lanes = [v[:, j * width : (j + 1) * width] for v in values]
            blocks.append(jnp.concatenate(lanes, 1).astype(BF))
    return dot(jnp.concatenate(blocks, 0), table_ref[...], ((1,), (0,)))


def update_kernel(pack, peers, *refs):
    back_refs, (point_ref, inverse_ref, forward_ref) = refs[:peers], refs[peers : peers + 3]
    state_ref, near_refs = refs[peers + 3], refs[peers + 4 :]
    count, rows, cells = state_ref.shape
    point = point_ref[...].reshape(count * rows, cells)
    updated = gelu(spread_of(pack, back_refs, inverse_ref) + point)
    state = updated.astype(BF)
    state_ref[...] = state.reshape(count, rows, cells)
    store_near(state, forward_ref[...], near_refs, pack, rows)


def last_kernel(pack, peers, first, kinds, *refs):
    back_refs = refs[:peers]
    me_ref, depth_ref, point_ref, inverse_ref, decoder_ref = refs[peers : peers + 5]
    updated_ref, *field_refs = refs[-kinds - 3 : -2]
    earlier = refs[peers + 5 : -kinds - 3]
    low_ref, high_ref = refs[-2:]
    count, rows, cells = updated_ref.shape
    group = pl.program_id(0)
    point = point_ref[...].reshape(count * rows, cells)
    updated = gelu(spread_of(pack, back_refs, inverse_ref) + point)
    updated_ref[...] = updated.reshape(count, rows, cells)

    @pl.when(group == 0)
    def _():
        for f in range(kinds):
            field_refs[f][...] = (
                earlier[1 + f][...] if earlier else jnp.zeros((rows, cells), F32)
            )

    lanes = next(b for b in (LANES, cells) if cells % b == 0)
    depth = depth_ref[me_ref[1]]
    weights = []
    for f in range(kinds):
        lines = [
            decoder_ref[pl.ds((first + group * count + c) * kinds + f, 1), :]
            for c in range(count)
        ]
        lines = [line * depth for line in lines] if f == kinds - 1 else lines
        weights.append([jnp.broadcast_to(line, (8, lanes)) for line in lines])

    def slab(t, carry):
        at = pl.ds(pl.multiple_of(t * 8, 8), 8)
        for start in range(0, cells, lanes):
            to = slice(start, start + lanes)
            values = [updated_ref[c, at, to] for c in range(count)]
            for f in range(kinds):
                terms = [weights[f][c] * values[c] for c in range(count)]
                while len(terms) > 1:
                    terms = [sum(terms[i + 1 : i + 2], terms[i]) for i in range(0, len(terms), 2)]
                field_refs[f][at, to] += terms[0]
        return carry

    lax.fori_loop(0, rows // 8, slab, 0)

    @pl.when(group == pl.num_programs(0) - 1)
    def _():
        for i, f in enumerate((1, kinds - 1)):
            low_ref[i : i + 1] = field_refs[f][:1]
            high_ref[i : i + 1] = field_refs[f][rows - 1 :]


def pair_kernel(me_ref, layer_ref, other_ref, rims_ref, other_rims_ref, both_ref):
    half = layer_ref.shape[0] // 2
    at = pl.ds(pl.multiple_of((me_ref[1] & 1) * half, 8), half)
    both_ref[:half] = layer_ref[at, :] + other_ref[at, :]
    both_ref[half : half + 2] = rims_ref[...] + other_rims_ref[...]
    both_ref[half + 2 :] = jnp.zeros((both_ref.shape[0] - half - 2, both_ref.shape[1]), F32)


def pointwise_kernel(chunks, block, *refs):
    state_refs, (forcing_ref, weight_ref, bias_ref, out_ref) = refs[:chunks], refs[chunks:]
    channels, rows, cells = out_ref.shape
    count = channels * block
    for t in range(rows // block):
        at = slice(t * block, (t + 1) * block)
        state = jnp.concatenate([ref[:, at] for ref in state_refs], 0).reshape(count, cells)
        source = forcing_ref[:, at].reshape(count, cells).astype(F32) + bias_ref[...]
        out = dot(weight_ref[...], state, ((1,), (0,))) + source
        out_ref[:, at] = out.reshape(channels, block, cells)


def residual_kernel(paired, *refs):
    east_ref, north_ref, upward_ref, layer_ref, below_ref, before_ref, after_ref = refs[:7]
    turning_ref, rims_ref, rest, out_ref = refs[7], refs[8], refs[9:-1], refs[-1]
    rows, cells = layer_ref.shape
    geopotential = layer_ref[...]
    rims = rims_ref[...]
    if paired:
        me_ref, other_ref, other_rims_ref, mine_ref, partner_ref = rest
        odd = (me_ref[1] & 1) == 1
        half = rows // 2
        mine, theirs = mine_ref[:half], partner_ref[:half]
        lower = jnp.concatenate(
            [jnp.where(odd, theirs, mine), jnp.where(odd, mine, theirs)], 0
        )
        geopotential = geopotential + jnp.where(odd, other_ref[...], 0.0) + lower
        rims = rims + jnp.where(odd, other_rims_ref[...], 0.0) + mine_ref[half : half + 2]
    else:
        count = len(rest) // 2
        for ref in rest[:count]:
            geopotential = geopotential + ref[...]
        for ref in rest[count:]:
            rims = rims + ref[...]
    rims = [rims[:1], rims[1:]]
    row = lax.broadcasted_iota(jnp.int32, (rows, cells), 0)

    def along_x(field):
        return (pltpu.roll(field, cells - 1, 1) - pltpu.roll(field, 1, 1)) * 0.5

    def along_y(field, first, last):
        later = jnp.where(row == rows - 1, last, pltpu.roll(field, rows - 1, 0))
        earlier = jnp.where(row == 0, first, pltpu.roll(field, 1, 0))
        return (later - earlier) * 0.5

    east, north, turning = east_ref[...], north_ref[...], turning_ref[...]
    north_y = along_y(north, before_ref[:1], after_ref[:1])
    out_ref[0] = along_x(east) + north_y + upward_ref[...] - below_ref[...]
    out_ref[1] = turning * north - along_x(geopotential)
    out_ref[2] = turning * east + along_y(geopotential, rims[0], rims[1])


def on_device(forcing, spectral_weight, point_weight, point_bias, decoder, coriolis, layer_depth):
    level_count, channels, rows, cells = forcing.shape
    assert level_count == 1
    forcing = forcing[0]
    slices = lax.axis_size("gy")
    peers = slices // 2
    own = spectral_weight.shape[1]
    modes = own * slices
    ymodes = spectral_weight.shape[4]
    total_rows = rows * slices
    pack = LANES // (4 * own)
    groups = channels // pack
    part = groups // CHUNKS
    size = channels // CHUNKS
    wide = peers * 4 * own
    me = jnp.stack([lax.axis_index("gy"), lax.axis_index("lev")]).astype(jnp.int32)

    forward_x, inverse_x = x_tables(cells, modes, slices, cells * total_rows)
    smem = pl.BlockSpec(memory_space=pltpu.SMEM)
    vmem = pl.BlockSpec(memory_space=pltpu.VMEM)

    def whole(shape):
        return pl.BlockSpec(shape, lambda i: (0,) * len(shape))

    def params(mib, *grid):
        return pltpu.CompilerParams(dimension_semantics=grid, vmem_limit_bytes=mib << 20)


    block = next(b for b in (16, 8, rows) if rows % b == 0)
    blocks = 1
    many = next(b for b in (4, 2, 1) if part % b == 0)

    near_table = pl.pallas_call(
        functools.partial(forward_table_kernel, own, peers),
        grid=(1,),
        in_specs=[smem, whole((cells, wide))],
        out_specs=whole((cells, wide)),
        out_shape=jax.ShapeDtypeStruct((cells, wide), BF),
        compiler_params=params(6, "arbitrary"),
        cost_estimate=cost(2 * cells * wide * wide, 4 * cells * wide),
        name="forward_table",
    )(me, jnp.asarray(forward_x))
    spread_table, row_table = pl.pallas_call(
        functools.partial(other_tables_kernel, own, peers),
        grid=(1,),
        in_specs=[smem, whole((wide, cells)), whole((slices, rows, 2 * ymodes))],
        out_specs=[whole((wide, cells)), whole((peers * rows, 2 * ymodes))],
        out_shape=[
            jax.ShapeDtypeStruct((wide, cells), BF),
            jax.ShapeDtypeStruct((peers * rows, 2 * ymodes), BF),
        ],
        compiler_params=params(8, "arbitrary"),
        cost_estimate=cost(2 * cells * wide * wide, 4 * cells * wide),
        name="other_tables",
    )(me, jnp.asarray(inverse_x), jnp.asarray(y_table(total_rows, ymodes, slices)))
    square, bias, decoder_splat = pl.pallas_call(
        functools.partial(small_kernel, block),
        in_specs=[vmem] * 3,
        out_specs=[vmem] * 3,
        out_shape=[
            jax.ShapeDtypeStruct((channels * block, channels * block), BF),
            jax.ShapeDtypeStruct((channels * block, 1), F32),
            jax.ShapeDtypeStruct((channels * decoder.shape[0], LANES), F32),
        ],
        compiler_params=params(8),
        cost_estimate=cost(2 * channels * (channels * block) ** 2, 1 << 20),
        name="small",
    )(point_weight, point_bias[None, :], decoder)

    def swap(value, distance):
        return lax.ppermute(value, "gy", [(g, g ^ distance) for g in range(slices)])

    cells_spec = pl.BlockSpec((many * pack, rows, cells), lambda i: (i, 0, 0))
    lane_spec = pl.BlockSpec((many, rows, LANES), lambda i: (i, 0, 0))
    lane_shape = jax.ShapeDtypeStruct((part, rows, LANES), BF)
    mode_spec = whole((size, own, 2 * ymodes))
    part_spec = whole((part, rows, LANES))
    tile = size * rows * cells

    def offset_spec(n):
        return pl.BlockSpec((many * pack, rows, cells), lambda i: (i + n * (part // many), 0, 0))

    def near_of(n):
        return pl.pallas_call(
            functools.partial(near_kernel, pack),
            grid=(part // many,),
            in_specs=[offset_spec(n), whole((cells, wide))],
            out_specs=[lane_spec] * peers,
            out_shape=[lane_shape] * peers,
            compiler_params=params(6, "arbitrary"),
            cost_estimate=cost(2 * tile * wide, tile * 2),
            name="near",
        )(pltpu.with_memory_space_constraint(forcing, pltpu.HBM), near_table)

    def exchange(parts):
        return [parts[0]] + [swap(parts[d], d) for d in range(1, peers)]

    def forward_y(parts):
        return pl.pallas_call(
            functools.partial(forward_y_kernel, pack, own, peers),
            grid=(1,),
            in_specs=[part_spec] * peers + [whole(row_table.shape)],
            out_specs=[mode_spec] * 2,
            out_shape=[
                jax.ShapeDtypeStruct((size, own, 2 * ymodes), F32),
                jax.ShapeDtypeStruct((size, own, 2 * ymodes), BF),
            ],
            compiler_params=params(8, "arbitrary"),
            cost_estimate=cost(4 * part * LANES * peers * rows * ymodes, 2 * size * rows * wide),
            name="forward_y",
        )(*parts, row_table)

    def mix(kept, got, n, earlier, outputs):
        count = outputs.stop - outputs.start
        final = n == CHUNKS - 1
        return pl.pallas_call(
            functools.partial(mix_kernel, n, CHUNKS, outputs),
            in_specs=[vmem] * (3 + len(earlier)),
            out_specs=vmem,
            out_shape=jax.ShapeDtypeStruct((count, own, 2 * ymodes), BF)
            if final
            else jax.ShapeDtypeStruct((own, count, 2 * ymodes), F32),
            scratch_shapes=[
                pltpu.VMEM((own, size, 2 * ymodes), F32),
                pltpu.VMEM((own, size, 2 * ymodes), F32),
            ],
            compiler_params=params(8),
            cost_estimate=cost(
                8 * own * count * size * ymodes, 4 * own * count * size * ymodes
            ),
            name="mix",
        )(kept, got, spectral_weight, *earlier)

    def inverse_y(mine, theirs):
        return pl.pallas_call(
            functools.partial(inverse_y_kernel, pack, peers),
            grid=(1,),
            in_specs=[mode_spec] * 2 + [whole(row_table.shape)],
            out_specs=[part_spec] * peers,
            out_shape=[lane_shape] * peers,
            compiler_params=params(8, "arbitrary"),
            cost_estimate=cost(4 * part * LANES * peers * rows * ymodes, 2 * size * rows * wide),
            name="inverse_y",
        )(mine, theirs, row_table)

    def pointwise(states):
        if len(states) == 1:
            specs = [pl.BlockSpec((channels, blocks * block, cells), lambda i: (0, i, 0))]
        else:
            specs = [pl.BlockSpec((size, blocks * block, cells), lambda i: (0, i, 0))] * CHUNKS
        return pl.pallas_call(
            functools.partial(pointwise_kernel, len(states), block),
            grid=(rows // (blocks * block),),
            in_specs=specs
            + [
                pl.BlockSpec((channels, blocks * block, cells), lambda i: (0, i, 0)),
                whole(square.shape),
                whole(bias.shape),
            ],
            out_specs=pl.BlockSpec((channels, blocks * block, cells), lambda i: (0, i, 0)),
            out_shape=jax.ShapeDtypeStruct((channels, rows, cells), F32),
            compiler_params=params(11, "arbitrary"),
            cost_estimate=cost(
                2 * channels * block * channels * rows * cells, 8 * channels * rows * cells
            ),
            name="pointwise",
        )(*states, forcing, square, bias)

    def update(backs, point, n):
        out = pl.pallas_call(
            functools.partial(update_kernel, pack, peers),
            grid=(part // many,),
            in_specs=[lane_spec] * peers
            + [offset_spec(n), whole(spread_table.shape), whole(near_table.shape)],
            out_specs=[cells_spec] + [lane_spec] * peers,
            out_shape=[jax.ShapeDtypeStruct((size, rows, cells), BF)] + [lane_shape] * peers,
            compiler_params=params(16, "arbitrary"),
            cost_estimate=cost(4 * tile * wide, 6 * tile, tile),
            name="update",
        )(*backs, point, spread_table, near_table)
        return out[0], out[1:]

    few = next(b for b in (2, 1) if part % b == 0)
    few_lanes = pl.BlockSpec((few, rows, LANES), lambda i: (i, 0, 0))

    def few_spec(n):
        return pl.BlockSpec(
            (few * pack, rows, cells), lambda i: (i + n * (part // few), 0, 0)
        )

    def last(backs, point, n, earlier):
        kinds = decoder.shape[0]
        more = [whole((rows, cells))] * kinds
        return pl.pallas_call(
            functools.partial(last_kernel, pack, peers, n * size, kinds),
            grid=(part // few,),
            in_specs=[few_lanes] * peers
            + [
                smem,
                smem,
                few_spec(n),
                whole(spread_table.shape),
                whole(decoder_splat.shape),
            ]
            + ([pl.BlockSpec(memory_space=pl.ANY)] + more if earlier else []),
            out_specs=[few_spec(n)] + more + [whole((2, cells))] * 2,
            out_shape=[jax.ShapeDtypeStruct((channels, rows, cells), F32)]
            + [jax.ShapeDtypeStruct((rows, cells), F32)] * kinds
            + [jax.ShapeDtypeStruct((2, cells), F32)] * 2,
            input_output_aliases={peers + 5: 0} if earlier else {},
            compiler_params=params(18, "arbitrary"),
            cost_estimate=cost(2 * tile * wide, 8 * tile, tile),
            name="last",
        )(*backs, me, layer_depth, point, spread_table, decoder_splat, *earlier[: kinds + 1])

    every = range(CHUNKS)
    nears = [near_of(n) for n in every]
    states = [forcing]
    for iteration in range(ITERS):
        arrived = [exchange(parts) for parts in nears]
        point = pointwise(states)
        halves = [forward_y(parts) for parts in arrived]
        kept = [half[0] for half in halves]
        got = [swap(half[1], peers) for half in halves]
        sums = []
        for n in range(CHUNKS - 1):
            sums = [mix(kept[n], got[n], n, sums, slice(0, channels))]
        mixed = [
            mix(kept[-1], got[-1], CHUNKS - 1, sums, slice(n * size, (n + 1) * size))
            for n in every
        ]
        theirs = []
        for n in every:
            theirs.append(swap(mixed[n], peers))
        backs = [exchange(inverse_y(mixed[n], theirs[n])) for n in every]
        if iteration < ITERS - 1:
            done = [update(backs[n], point, n) for n in every]
            states = [pair[0] for pair in done]
            nears = [pair[1] for pair in done]
    done = []
    for n in every:
        done = last(backs[n], point, n, done)
    updated, east, north, upward, layer, low, high = done

    levels = lax.axis_size("lev")

    def from_below(value, step):
        return lax.ppermute(value, "lev", [(s, s + step) for s in range(levels - step)])

    up = [(i, (i + 1) % slices) for i in range(slices)]
    down = [(j, i) for i, j in up]
    pairs = levels % 2 == 0 and rows % 16 == 0
    if pairs:
        partner = [(s, s ^ 1) for s in range(levels)]
        other = lax.ppermute(layer, "lev", partner)
    below = from_below(upward, 1)
    before = lax.ppermute(high, "gy", up)
    after = lax.ppermute(low, "gy", down)
    rims = jnp.concatenate([before[1:], after[1:]], 0)
    if pairs:
        other_rims = lax.ppermute(rims, "lev", partner)
        both = pl.pallas_call(
            pair_kernel,
            in_specs=[smem] + [vmem] * 4,
            out_specs=vmem,
            out_shape=jax.ShapeDtypeStruct((rows // 2 + 8, cells), F32),
            compiler_params=params(2),
            cost_estimate=cost(rows * cells, 8 * rows * cells),
            name="pair",
        )(me, layer, other, rims, other_rims)
        lower = from_below(both, 2)
        step = 2
        while step < levels - 2:
            lower = lower + from_below(lower, step)
            step *= 2
        lowers = [me, other, other_rims, lower, lax.ppermute(lower, "lev", partner)]
    else:
        lowers = [from_below(v, step) for v in (layer, rims) for step in range(1, levels)]
    residual = pl.pallas_call(
        functools.partial(residual_kernel, pairs),
        in_specs=[vmem] * 9
        + ([smem] if pairs else [vmem])
        + [vmem] * (len(lowers) - 1),
        out_specs=vmem,
        out_shape=jax.ShapeDtypeStruct((3, rows, cells), F32),
        compiler_params=params(10),
        cost_estimate=cost(20 * rows * cells, 36 * rows * cells),
        name="residual",
    )(
        east,
        north,
        upward,
        layer,
        below,
        before,
        after,
        coriolis[:, None],
        rims,
        *lowers,
    )
    return updated[None], residual[:, None]


def solution(mesh):
    return jax.shard_map(
        on_device,
        mesh=mesh,
        in_specs=(
            P("lev", None, "gy", None),
            P(None, "gy", None, None, None),
            P(),
            P(),
            P(),
            P("gy"),
            P(),
        ),
        out_specs=(P("lev", None, "gy", None), P(None, "lev", "gy", None)),
        check_vma=False,
    )
```

```python
import functools
import math

import jax
import jax.numpy as jnp
import numpy as np
from jax import lax
from jax.experimental import pallas as pl
from jax.experimental.pallas import tpu as pltpu
from jax.sharding import PartitionSpec as P


ITERS = 3
CHUNKS = 2
BF = jnp.bfloat16
F32 = jnp.float32
LANES = 128


def cost(flops, bytes_accessed, transcendentals=0):
    return pl.CostEstimate(
        flops=int(flops), bytes_accessed=int(bytes_accessed), transcendentals=int(transcendentals)
    )


def turned(rows, cols, length):
    phase = (rows[:, None] * cols[None, :]) % length
    return phase.astype(np.float32) * np.float32(2.0 * math.pi / length)


def x_tables(cells, modes, slices, total):
    angle = turned(np.arange(modes, dtype=np.int64), np.arange(cells, dtype=np.int64), cells)
    pair = np.stack([np.cos(angle), -np.sin(angle)], 0).astype(np.float32)
    factor = (np.where(np.arange(modes) == 0, 1.0, 2.0).astype(np.float32) / np.float32(total))
    inverse = pair * factor[None, :, None] * np.float32(0.5)
    own = modes // slices

    def by_slice(table):
        table = table.reshape(2, slices, own, cells).transpose(1, 0, 2, 3)
        return table.reshape(slices, 2 * own, cells).astype(BF)

    order = [d + h * (slices // 2) for d in range(slices // 2) for h in range(2)]
    first, second = [by_slice(table)[order].reshape(-1, cells) for table in (pair, inverse)]
    return np.ascontiguousarray(first.T), second


def y_table(rows, modes, slices):
    index = np.arange(modes, dtype=np.int64)
    signed = np.where(index < modes // 2, index, index + (rows - modes))
    angle = turned(np.arange(rows, dtype=np.int64), signed, rows)
    both = np.concatenate([np.cos(angle), np.sin(angle)], 1).astype(np.float32)
    return both.reshape(slices, rows // slices, 2 * modes).astype(BF)


def dot(a, b, dims):
    return lax.dot_general(a, b, (dims, ((), ())), preferred_element_type=F32)


def store_near(state, table, near_refs, pack, rows, first=0):
    width = LANES // pack
    near = dot(state, table, ((1,), (0,)))
    for g in range(state.shape[0] // (pack * rows)):
        for d, ref in enumerate(near_refs):
            parts = []
            for j in range(pack):
                at = (g * pack + j) * rows
                parts.append(near[at : at + rows, d * width : (d + 1) * width])
            ref[first + g] = jnp.concatenate(parts, 1).astype(BF)


def near_kernel(pack, state_ref, table_ref, *near_refs):
    count, rows, cells = state_ref.shape
    state = state_ref[...].reshape(count * rows, cells)
    store_near(state, table_ref[...], near_refs, pack, rows)


def slice_order(own, peers, me, across, along):
    wide = peers * 4 * own
    block = 2 * own
    mask = ((me % peers) * 2) | (me // peers)
    place = lax.broadcasted_iota(jnp.int32, (wide, wide), across)
    source = ((place // block) ^ mask) * block + place % block
    return (lax.broadcasted_iota(jnp.int32, (wide, wide), along) == source).astype(BF)


def forward_table_kernel(own, peers, me_ref, forward_ref, near_ref):
    order = slice_order(own, peers, me_ref[0], 1, 0)
    near_ref[...] = dot(forward_ref[...], order, ((1,), (0,))).astype(BF)


def other_tables_kernel(own, peers, me_ref, inverse_ref, row_ref, spread_ref, rows_ref):
    order = slice_order(own, peers, me_ref[0], 0, 1)
    spread_ref[...] = dot(order, inverse_ref[...], ((1,), (0,))).astype(BF)
    rows = row_ref.shape[1]
    for d in range(peers):
        rows_ref[d * rows : (d + 1) * rows] = row_ref[me_ref[0] ^ d]


def small_kernel(block, weight_ref, bias_ref, decoder_ref, square_ref, column_ref, splat_ref):
    channels = weight_ref.shape[0]
    count = channels * block
    row = lax.broadcasted_iota(jnp.int32, (count, channels), 0) // block
    mine = row == lax.broadcasted_iota(jnp.int32, (count, channels), 1)
    pick = mine.astype(BF)
    left = dot(pick, weight_ref[...], ((1,), (1,))).astype(BF)
    full = dot(left, pick, ((1,), (1,)))
    down = lax.broadcasted_iota(jnp.int32, (count, count), 0) % block
    across = lax.broadcasted_iota(jnp.int32, (count, count), 1) % block
    square_ref[...] = jnp.where(down == across, 0.5 * full, 0.0).astype(BF)
    column_ref[...] = 0.5 * jnp.sum(jnp.where(mine, bias_ref[...], 0.0), 1, keepdims=True)
    fields = decoder_ref.shape[0]
    lines = channels * fields
    row = lax.broadcasted_iota(jnp.int32, (lines, channels), 0) // fields
    pick = (row == lax.broadcasted_iota(jnp.int32, (lines, channels), 1)).astype(BF)
    values = dot(pick, decoder_ref[...], ((1,), (1,)))
    row = lax.broadcasted_iota(jnp.int32, (lines, fields), 0) % fields
    own = row == lax.broadcasted_iota(jnp.int32, (lines, fields), 1)
    value = jnp.sum(jnp.where(own, values, 0.0), 1, keepdims=True)
    splat_ref[...] = jnp.broadcast_to(value, splat_ref.shape)


def forward_y_kernel(pack, own, peers, *refs):
    near_refs, (table_ref, keep_ref, send_ref) = refs[:peers], refs[peers:]
    modes = table_ref.shape[1] // 2
    for g in range(near_refs[0].shape[0]):
        near = jnp.concatenate([ref[g] for ref in near_refs], 0)
        both = dot(near, table_ref[...], ((0,), (0,)))
        for j in range(pack):
            for h, out_ref in ((0, keep_ref), (1, send_ref)):
                at = (j * 2 + h) * 2 * own
                real = both[at : at + own]
                imag = both[at + own : at + 2 * own]
                c = g * pack + j
                out_ref[c, :, :modes] = (real[:, :modes] + imag[:, modes:]).astype(out_ref.dtype)
                out_ref[c, :, modes:] = (imag[:, :modes] - real[:, modes:]).astype(out_ref.dtype)


def mix_kernel(n, chunks, outputs, *refs):
    keep_ref, got_ref, weight_ref = refs[:3]
    earlier_ref = refs[3] if n > 0 else None
    out_ref, spectrum, mixed = refs[-3:]
    own, channels, modes = weight_ref.shape[1], weight_ref.shape[2], weight_ref.shape[4]
    size = channels // chunks
    value = keep_ref[...] + got_ref[...].astype(F32)
    spectrum[...] = jnp.swapaxes(value, 0, 1)
    final = n == chunks - 1
    total = mixed if final else out_ref

    def step(k, carry):
        row = spectrum[k]
        zero = jnp.zeros((outputs.stop - outputs.start, modes), F32)
        real, imag = [zero, zero], [zero, zero]
        if n > 0:
            real[0] = earlier_ref[k, outputs, :modes]
            imag[0] = earlier_ref[k, outputs, modes:]
        for i in range(size):
            s0, s1 = row[i : i + 1, :modes], row[i : i + 1, modes:]
            w0 = weight_ref[0, k, n * size + i, outputs].astype(F32)
            w1 = weight_ref[1, k, n * size + i, outputs].astype(F32)
            real[i % 2] = real[i % 2] + (s0 * w0 - s1 * w1)
            imag[i % 2] = imag[i % 2] + (s0 * w1 + s1 * w0)
        total[k, :, :modes] = real[0] + real[1]
        total[k, :, modes:] = imag[0] + imag[1]
        return carry

    lax.fori_loop(0, own, step, 0)
    if final:
        out_ref[...] = jnp.swapaxes(mixed[...], 0, 1).astype(BF)


def inverse_y_kernel(pack, peers, mine_ref, theirs_ref, table_ref, *back_refs):
    rows, modes = table_ref.shape[0] // peers, table_ref.shape[1] // 2
    for g in range(back_refs[0].shape[0]):
        parts = []
        for j in range(pack):
            for ref in (mine_ref, theirs_ref):
                value = ref[g * pack + j].astype(F32)
                real, imag = value[:, :modes], value[:, modes:]
                parts.append(jnp.concatenate([real, -imag], 1))
                parts.append(jnp.concatenate([imag, real], 1))
        turned_modes = jnp.concatenate(parts, 0).astype(BF)
        back = dot(table_ref[...], turned_modes, ((1,), (1,)))
        for d in range(peers):
            back_refs[d][g] = back[d * rows : (d + 1) * rows].astype(BF)


def gelu(half):
    scale = 2.0 * math.sqrt(2.0 / math.pi)
    return half + half * jnp.tanh(half * (scale + (scale * 4.0 * 0.044715) * (half * half)))


def spread_of(pack, back_refs, table_ref):
    width = LANES // pack
    blocks = []
    for g in range(back_refs[0].shape[0]):
        values = [ref[g].astype(F32) for ref in back_refs]
        for j in range(pack):
            lanes = [v[:, j * width : (j + 1) * width] for v in values]
            blocks.append(jnp.concatenate(lanes, 1).astype(BF))
    return dot(jnp.concatenate(blocks, 0), table_ref[...], ((1,), (0,)))


def update_kernel(pack, peers, *refs):
    back_refs, (point_ref, inverse_ref, forward_ref) = refs[:peers], refs[peers : peers + 3]
    state_ref, near_refs = refs[peers + 3], refs[peers + 4 :]
    count, rows, cells = state_ref.shape
    point = point_ref[...].reshape(count * rows, cells)
    updated = gelu(spread_of(pack, back_refs, inverse_ref) + point)
    state = updated.astype(BF)
    state_ref[...] = state.reshape(count, rows, cells)
    store_near(state, forward_ref[...], near_refs, pack, rows)


def last_kernel(pack, peers, first, kinds, *refs):
    back_refs = refs[:peers]
    me_ref, depth_ref, point_ref, inverse_ref, decoder_ref = refs[peers : peers + 5]
    updated_ref, *field_refs = refs[-kinds - 3 : -2]
    earlier = refs[peers + 5 : -kinds - 3]
    low_ref, high_ref = refs[-2:]
    count, rows, cells = updated_ref.shape
    group = pl.program_id(0)
    point = point_ref[...].reshape(count * rows, cells)
    updated = gelu(spread_of(pack, back_refs, inverse_ref) + point)
    updated_ref[...] = updated.reshape(count, rows, cells)

    @pl.when(group == 0)
    def _():
        for f in range(kinds):
            field_refs[f][...] = (
                earlier[1 + f][...] if earlier else jnp.zeros((rows, cells), F32)
            )

    lanes = next(b for b in (LANES, cells) if cells % b == 0)
    depth = depth_ref[me_ref[1]]
    weights = []
    for f in range(kinds):
        lines = [
            decoder_ref[pl.ds((first + group * count + c) * kinds + f, 1), :]
            for c in range(count)
        ]
        lines = [line * depth for line in lines] if f == kinds - 1 else lines
        weights.append([jnp.broadcast_to(line, (8, lanes)) for line in lines])

    def slab(t, carry):
        at = pl.ds(pl.multiple_of(t * 8, 8), 8)
        for start in range(0, cells, lanes):
            to = slice(start, start + lanes)
            values = [updated_ref[c, at, to] for c in range(count)]
            for f in range(kinds):
                terms = [weights[f][c] * values[c] for c in range(count)]
                while len(terms) > 1:
                    terms = [sum(terms[i + 1 : i + 2], terms[i]) for i in range(0, len(terms), 2)]
                field_refs[f][at, to] += terms[0]
        return carry

    lax.fori_loop(0, rows // 8, slab, 0)

    @pl.when(group == pl.num_programs(0) - 1)
    def _():
        for i, f in enumerate((1, kinds - 1)):
            low_ref[i : i + 1] = field_refs[f][:1]
            high_ref[i : i + 1] = field_refs[f][rows - 1 :]


def pair_kernel(me_ref, layer_ref, other_ref, rims_ref, other_rims_ref, both_ref):
    half = layer_ref.shape[0] // 2
    at = pl.ds(pl.multiple_of((me_ref[1] & 1) * half, 8), half)
    both_ref[:half] = layer_ref[at, :] + other_ref[at, :]
    both_ref[half : half + 2] = rims_ref[...] + other_rims_ref[...]
    both_ref[half + 2 :] = jnp.zeros((both_ref.shape[0] - half - 2, both_ref.shape[1]), F32)


def pointwise_kernel(chunks, block, *refs):
    state_refs, (forcing_ref, weight_ref, bias_ref, out_ref) = refs[:chunks], refs[chunks:]
    channels, rows, cells = out_ref.shape
    count = channels * block
    for t in range(rows // block):
        at = slice(t * block, (t + 1) * block)
        state = jnp.concatenate([ref[:, at] for ref in state_refs], 0).reshape(count, cells)
        source = 0.5 * forcing_ref[:, at].reshape(count, cells).astype(F32) + bias_ref[...]
        out = dot(weight_ref[...], state, ((1,), (0,))) + source
        out_ref[:, at] = out.reshape(channels, block, cells)


def residual_kernel(paired, *refs):
    east_ref, north_ref, upward_ref, layer_ref, below_ref, before_ref, after_ref = refs[:7]
    turning_ref, rims_ref, rest, out_ref = refs[7], refs[8], refs[9:-1], refs[-1]
    rows, cells = layer_ref.shape
    geopotential = layer_ref[...]
    rims = rims_ref[...]
    if paired:
        me_ref, other_ref, other_rims_ref, mine_ref, partner_ref = rest
        odd = (me_ref[1] & 1) == 1
        half = rows // 2
        mine, theirs = mine_ref[:half], partner_ref[:half]
        lower = jnp.concatenate(
            [jnp.where(odd, theirs, mine), jnp.where(odd, mine, theirs)], 0
        )
        geopotential = geopotential + jnp.where(odd, other_ref[...], 0.0) + lower
        rims = rims + jnp.where(odd, other_rims_ref[...], 0.0) + mine_ref[half : half + 2]
    else:
        count = len(rest) // 2
        for ref in rest[:count]:
            geopotential = geopotential + ref[...]
        for ref in rest[count:]:
            rims = rims + ref[...]
    rims = [rims[:1], rims[1:]]
    row = lax.broadcasted_iota(jnp.int32, (rows, cells), 0)

    def along_x(field):
        return (pltpu.roll(field, cells - 1, 1) - pltpu.roll(field, 1, 1)) * 0.5

    def along_y(field, first, last):
        later = jnp.where(row == rows - 1, last, pltpu.roll(field, rows - 1, 0))
        earlier = jnp.where(row == 0, first, pltpu.roll(field, 1, 0))
        return (later - earlier) * 0.5

    east, north, turning = east_ref[...], north_ref[...], turning_ref[...]
    north_y = along_y(north, before_ref[:1], after_ref[:1])
    out_ref[0] = along_x(east) + north_y + upward_ref[...] - below_ref[...]
    out_ref[1] = turning * north - along_x(geopotential)
    out_ref[2] = turning * east + along_y(geopotential, rims[0], rims[1])


def on_device(forcing, spectral_weight, point_weight, point_bias, decoder, coriolis, layer_depth):
    level_count, channels, rows, cells = forcing.shape
    assert level_count == 1
    forcing = forcing[0]
    slices = lax.axis_size("gy")
    peers = slices // 2
    own = spectral_weight.shape[1]
    modes = own * slices
    ymodes = spectral_weight.shape[4]
    total_rows = rows * slices
    pack = LANES // (4 * own)
    groups = channels // pack
    part = groups // CHUNKS
    size = channels // CHUNKS
    wide = peers * 4 * own
    me = jnp.stack([lax.axis_index("gy"), lax.axis_index("lev")]).astype(jnp.int32)

    forward_x, inverse_x = x_tables(cells, modes, slices, cells * total_rows)
    smem = pl.BlockSpec(memory_space=pltpu.SMEM)
    vmem = pl.BlockSpec(memory_space=pltpu.VMEM)

    def whole(shape):
        return pl.BlockSpec(shape, lambda i: (0,) * len(shape))

    def params(mib, *grid):
        return pltpu.CompilerParams(dimension_semantics=grid, vmem_limit_bytes=mib << 20)


    block = next(b for b in (16, 8, rows) if rows % b == 0)
    blocks = 1
    many = next(b for b in (4, 2, 1) if part % b == 0)

    near_table = pl.pallas_call(
        functools.partial(forward_table_kernel, own, peers),
        grid=(1,),
        in_specs=[smem, whole((cells, wide))],
        out_specs=whole((cells, wide)),
        out_shape=jax.ShapeDtypeStruct((cells, wide), BF),
        compiler_params=params(6, "arbitrary"),
        cost_estimate=cost(2 * cells * wide * wide, 4 * cells * wide),
        name="forward_table",
    )(me, jnp.asarray(forward_x))
    spread_table, row_table = pl.pallas_call(
        functools.partial(other_tables_kernel, own, peers),
        grid=(1,),
        in_specs=[smem, whole((wide, cells)), whole((slices, rows, 2 * ymodes))],
        out_specs=[whole((wide, cells)), whole((peers * rows, 2 * ymodes))],
        out_shape=[
            jax.ShapeDtypeStruct((wide, cells), BF),
            jax.ShapeDtypeStruct((peers * rows, 2 * ymodes), BF),
        ],
        compiler_params=params(8, "arbitrary"),
        cost_estimate=cost(2 * cells * wide * wide, 4 * cells * wide),
        name="other_tables",
    )(me, jnp.asarray(inverse_x), jnp.asarray(y_table(total_rows, ymodes, slices)))
    square, bias, decoder_splat = pl.pallas_call(
        functools.partial(small_kernel, block),
        in_specs=[vmem] * 3,
        out_specs=[vmem] * 3,
        out_shape=[
            jax.ShapeDtypeStruct((channels * block, channels * block), BF),
            jax.ShapeDtypeStruct((channels * block, 1), F32),
            jax.ShapeDtypeStruct((channels * decoder.shape[0], LANES), F32),
        ],
        compiler_params=params(8),
        cost_estimate=cost(2 * channels * (channels * block) ** 2, 1 << 20),
        name="small",
    )(point_weight, point_bias[None, :], decoder)

    def swap(value, distance):
        return lax.ppermute(value, "gy", [(g, g ^ distance) for g in range(slices)])

    cells_spec = pl.BlockSpec((many * pack, rows, cells), lambda i: (i, 0, 0))
    lane_spec = pl.BlockSpec((many, rows, LANES), lambda i: (i, 0, 0))
    lane_shape = jax.ShapeDtypeStruct((part, rows, LANES), BF)
    mode_spec = whole((size, own, 2 * ymodes))
    part_spec = whole((part, rows, LANES))
    tile = size * rows * cells

    def offset_spec(n):
        return pl.BlockSpec((many * pack, rows, cells), lambda i: (i + n * (part // many), 0, 0))

    def near_of(n):
        return pl.pallas_call(
            functools.partial(near_kernel, pack),
            grid=(part // many,),
            in_specs=[offset_spec(n), whole((cells, wide))],
            out_specs=[lane_spec] * peers,
            out_shape=[lane_shape] * peers,
            compiler_params=params(6, "arbitrary"),
            cost_estimate=cost(2 * tile * wide, tile * 2),
            name="near",
        )(pltpu.with_memory_space_constraint(forcing, pltpu.HBM), near_table)

    def exchange(parts):
        return [parts[0]] + [swap(parts[d], d) for d in range(1, peers)]

    def forward_y(parts):
        return pl.pallas_call(
            functools.partial(forward_y_kernel, pack, own, peers),
            grid=(1,),
            in_specs=[part_spec] * peers + [whole(row_table.shape)],
            out_specs=[mode_spec] * 2,
            out_shape=[
                jax.ShapeDtypeStruct((size, own, 2 * ymodes), F32),
                jax.ShapeDtypeStruct((size, own, 2 * ymodes), BF),
            ],
            compiler_params=params(8, "arbitrary"),
            cost_estimate=cost(4 * part * LANES * peers * rows * ymodes, 2 * size * rows * wide),
            name="forward_y",
        )(*parts, row_table)

    def mix(kept, got, n, earlier, outputs):
        count = outputs.stop - outputs.start
        final = n == CHUNKS - 1
        return pl.pallas_call(
            functools.partial(mix_kernel, n, CHUNKS, outputs),
            in_specs=[vmem] * (3 + len(earlier)),
            out_specs=vmem,
            out_shape=jax.ShapeDtypeStruct((count, own, 2 * ymodes), BF)
            if final
            else jax.ShapeDtypeStruct((own, count, 2 * ymodes), F32),
            scratch_shapes=[
                pltpu.VMEM((own, size, 2 * ymodes), F32),
                pltpu.VMEM((own, size, 2 * ymodes), F32),
            ],
            compiler_params=params(8),
            cost_estimate=cost(
                8 * own * count * size * ymodes, 4 * own * count * size * ymodes
            ),
            name="mix",
        )(kept, got, spectral_weight, *earlier)

    def inverse_y(mine, theirs):
        return pl.pallas_call(
            functools.partial(inverse_y_kernel, pack, peers),
            grid=(1,),
            in_specs=[mode_spec] * 2 + [whole(row_table.shape)],
            out_specs=[part_spec] * peers,
            out_shape=[lane_shape] * peers,
            compiler_params=params(8, "arbitrary"),
            cost_estimate=cost(4 * part * LANES * peers * rows * ymodes, 2 * size * rows * wide),
            name="inverse_y",
        )(mine, theirs, row_table)

    def pointwise(states):
        if len(states) == 1:
            specs = [pl.BlockSpec((channels, blocks * block, cells), lambda i: (0, i, 0))]
        else:
            specs = [pl.BlockSpec((size, blocks * block, cells), lambda i: (0, i, 0))] * CHUNKS
        return pl.pallas_call(
            functools.partial(pointwise_kernel, len(states), block),
            grid=(rows // (blocks * block),),
            in_specs=specs
            + [
                pl.BlockSpec((channels, blocks * block, cells), lambda i: (0, i, 0)),
                whole(square.shape),
                whole(bias.shape),
            ],
            out_specs=pl.BlockSpec((channels, blocks * block, cells), lambda i: (0, i, 0)),
            out_shape=jax.ShapeDtypeStruct((channels, rows, cells), F32),
            compiler_params=params(11, "arbitrary"),
            cost_estimate=cost(
                2 * channels * block * channels * rows * cells, 8 * channels * rows * cells
            ),
            name="pointwise",
        )(*states, forcing, square, bias)

    def update(backs, point, n):
        out = pl.pallas_call(
            functools.partial(update_kernel, pack, peers),
            grid=(part // many,),
            in_specs=[lane_spec] * peers
            + [offset_spec(n), whole(spread_table.shape), whole(near_table.shape)],
            out_specs=[cells_spec] + [lane_spec] * peers,
            out_shape=[jax.ShapeDtypeStruct((size, rows, cells), BF)] + [lane_shape] * peers,
            compiler_params=params(16, "arbitrary"),
            cost_estimate=cost(4 * tile * wide, 6 * tile, tile),
            name="update",
        )(*backs, point, spread_table, near_table)
        return out[0], out[1:]

    few = next(b for b in (2, 1) if part % b == 0)
    few_lanes = pl.BlockSpec((few, rows, LANES), lambda i: (i, 0, 0))

    def few_spec(n):
        return pl.BlockSpec(
            (few * pack, rows, cells), lambda i: (i + n * (part // few), 0, 0)
        )

    def last(backs, point, n, earlier):
        kinds = decoder.shape[0]
        more = [whole((rows, cells))] * kinds
        return pl.pallas_call(
            functools.partial(last_kernel, pack, peers, n * size, kinds),
            grid=(part // few,),
            in_specs=[few_lanes] * peers
            + [
                smem,
                smem,
                few_spec(n),
                whole(spread_table.shape),
                whole(decoder_splat.shape),
            ]
            + ([pl.BlockSpec(memory_space=pl.ANY)] + more if earlier else []),
            out_specs=[few_spec(n)] + more + [whole((2, cells))] * 2,
            out_shape=[jax.ShapeDtypeStruct((channels, rows, cells), F32)]
            + [jax.ShapeDtypeStruct((rows, cells), F32)] * kinds
            + [jax.ShapeDtypeStruct((2, cells), F32)] * 2,
            input_output_aliases={peers + 5: 0} if earlier else {},
            compiler_params=params(18, "arbitrary"),
            cost_estimate=cost(2 * tile * wide, 8 * tile, tile),
            name="last",
        )(*backs, me, layer_depth, point, spread_table, decoder_splat, *earlier[: kinds + 1])

    every = range(CHUNKS)
    nears = [near_of(n) for n in every]
    states = [forcing]
    for iteration in range(ITERS):
        arrived = [exchange(parts) for parts in nears]
        point = pointwise(states)
        halves = [forward_y(parts) for parts in arrived]
        kept = [half[0] for half in halves]
        got = [swap(half[1], peers) for half in halves]
        sums = []
        for n in range(CHUNKS - 1):
            sums = [mix(kept[n], got[n], n, sums, slice(0, channels))]
        mixed = [
            mix(kept[-1], got[-1], CHUNKS - 1, sums, slice(n * size, (n + 1) * size))
            for n in every
        ]
        theirs = []
        for n in every:
            theirs.append(swap(mixed[n], peers))
        backs = [exchange(inverse_y(mixed[n], theirs[n])) for n in every]
        if iteration < ITERS - 1:
            done = [update(backs[n], point, n) for n in every]
            states = [pair[0] for pair in done]
            nears = [pair[1] for pair in done]
    done = []
    for n in every:
        done = last(backs[n], point, n, done)
    updated, east, north, upward, layer, low, high = done

    levels = lax.axis_size("lev")

    def from_below(value, step):
        return lax.ppermute(value, "lev", [(s, s + step) for s in range(levels - step)])

    up = [(i, (i + 1) % slices) for i in range(slices)]
    down = [(j, i) for i, j in up]
    pairs = levels % 2 == 0 and rows % 16 == 0
    if pairs:
        partner = [(s, s ^ 1) for s in range(levels)]
        other = lax.ppermute(layer, "lev", partner)
    below = from_below(upward, 1)
    before = lax.ppermute(high, "gy", up)
    after = lax.ppermute(low, "gy", down)
    rims = jnp.concatenate([before[1:], after[1:]], 0)
    if pairs:
        other_rims = lax.ppermute(rims, "lev", partner)
        both = pl.pallas_call(
            pair_kernel,
            in_specs=[smem] + [vmem] * 4,
            out_specs=vmem,
            out_shape=jax.ShapeDtypeStruct((rows // 2 + 8, cells), F32),
            compiler_params=params(2),
            cost_estimate=cost(rows * cells, 8 * rows * cells),
            name="pair",
        )(me, layer, other, rims, other_rims)
        lower = from_below(both, 2)
        step = 2
        while step < levels - 2:
            lower = lower + from_below(lower, step)
            step *= 2
        lowers = [me, other, other_rims, lower, lax.ppermute(lower, "lev", partner)]
    else:
        lowers = [from_below(v, step) for v in (layer, rims) for step in range(1, levels)]
    residual = pl.pallas_call(
        functools.partial(residual_kernel, pairs),
        in_specs=[vmem] * 9
        + ([smem] if pairs else [vmem])
        + [vmem] * (len(lowers) - 1),
        out_specs=vmem,
        out_shape=jax.ShapeDtypeStruct((3, rows, cells), F32),
        compiler_params=params(10),
        cost_estimate=cost(20 * rows * cells, 36 * rows * cells),
        name="residual",
    )(
        east,
        north,
        upward,
        layer,
        below,
        before,
        after,
        coriolis[:, None],
        rims,
        *lowers,
    )
    return updated[None], residual[:, None]


def solution(mesh):
    return jax.shard_map(
        on_device,
        mesh=mesh,
        in_specs=(
            P("lev", None, "gy", None),
            P(None, "gy", None, None, None),
            P(),
            P(),
            P(),
            P("gy"),
            P(),
        ),
        out_specs=(P("lev", None, "gy", None), P(None, "lev", "gy", None)),
        check_vma=False,
    )
```
